256 devices in a mesh: dp: 16 (over z, core), expert: 16 (over y, x).
Axes of the slice: x: 4, y: 4, z: 8, core: 2. Of those that a mesh axis runs over, the one named last changes fastest.
Arguments:
- cotangent: bfloat16 [32768, 2048], P(('dp', 'expert')), may hold values from -6 to 6
- saved_gate_up: bfloat16 [32768, 8, 1536], P(('dp', 'expert')), may hold values from -6 to 6
- route_ids: int32 [32768, 8], P(('dp', 'expert')), may hold values from 0 to 31, all different within a row; in each aligned block of 128 rows (0 to 127, 128 to 255, ...) at most 64 rows name the same one
- route_weights: float32 [32768, 8], P(('dp', 'expert')), may hold values from 0.05 to 1
- w_down: bfloat16 [32, 768, 2048], P('expert', 'dp'), may hold values from -0.21875 to 0.21875
Outputs:
- grad_gate_up: bfloat16 [32768, 8, 1536], P(('dp', 'expert'))
- route_grad: float32 [32768, 8], P(('dp', 'expert'))
- grad_down: float32 [32, 768, 2048], P('expert', 'dp')
The draws below stay inside these ranges and needn't reach their ends.
Inputs may be any that keep to these rules, and one draw needn't show every extreme that they name: `route_ids`: within the rows of one device (aligned blocks of 128 tokens), no expert is named by more than 64 routes, and in every draw some expert is named by exactly 64; the 8 experts of a token are distinct.
All inputs are finite; a program needn't handle non-finite values.
Results may differ from the reference program's by a relative error of at most 0.02.
Values may be sent and summed in bfloat16 or wider, within the bound.
A program may use at most 128 MiB of HBM per device.

```python
import math
import jax
import jax.numpy as jnp
import numpy as np
from jax import lax

D = 2048
FF = 768
TOP = 8
TOK_DEV = 128
EXPERTS = 32
CAP = 64
TOKENS = 32768
N_DP = 16
N_EXPERT = 16


def steps_of(own_key, dims, pieces, smallest, high):
    gain = 1.0
    for dim, blocks in pieces:
        draws = jax.random.uniform(jax.random.fold_in(jax.random.fold_in(own_key, 6), dim), (blocks,), jnp.float32, smallest / len(pieces), high / len(pieces))
        gain = gain * jnp.repeat(jnp.exp(draws), dims[dim] // blocks).reshape((-1,) + (1,) * (len(dims) - 1 - dim))
    return gain


def assign_block(rng, own, number, rows, amount, top, bound, skew):
    order = jax.random.permutation(rng, amount)
    heavy_load, common = shares(amount, rows * top, bound, skew, True), shares(amount, rows * top, bound, skew, False)
    places = jnp.arange(amount)

    def named(sizes, offset_by):
        used = int((sizes > 0).sum())
        fixed = max(1, used // 4)
        shifted = fixed + (places - fixed + offset_by * (used - fixed)) % max(1, amount - fixed)
        return jnp.zeros((amount,), jnp.int32).at[order[jnp.where(places < fixed, places, shifted)]].set(jnp.asarray(sizes, jnp.int32))

    sizes = jnp.where(number % 4 == 0, named(heavy_load, number // 4), named(common, number - number // 4 - 1))
    mixed = jax.random.permutation(jax.random.fold_in(own, 3), amount)
    source_of, taker = mixed[0:amount // 2 * 2:2], mixed[1:amount // 2 * 2:2]
    margin = jnp.minimum(sizes[source_of] - 1, bound - sizes[taker]) // 2
    margin = jnp.where((source_of == order[0]) | (taker == order[0]) | (sizes[taker] == 0), 0, jnp.maximum(margin, 0))
    shifted = jax.random.randint(jax.random.fold_in(own, 4), (amount // 2,), 0, 1 << 20) % (margin + 1)
    sizes = sizes.at[source_of].add(-shifted).at[taker].add(shifted)
    items = jnp.searchsorted(jnp.cumsum(sizes), jnp.arange(rows * top), side="right").astype(jnp.int32)
    grid = items.reshape(top, rows).T
    grid = grid[jax.random.permutation(jax.random.fold_in(own, 1), rows)]
    offset_by = jax.random.randint(jax.random.fold_in(own, 2), (rows, 1), 0, top)
    return jnp.take_along_axis(grid, (jnp.arange(top)[None, :] + offset_by) % top, axis=1)


def shares(count, total, limit, skew, full):
    weights = [(1 << 20) // math.isqrt(grade ** skew) + 1 for grade in range(1, count + 1)]
    largest = limit if full else min(limit, max(-(-total // count), total * weights[0] // sum(weights)))
    least = 1 if total - largest >= count - 1 else 0
    given, spare = [largest] + [least] * (count - 1), total - largest - least * (count - 1)
    while spare > 0:
        candidates = [i for i in range(1, count) if given[i] < largest] or [i for i in range(1, count) if given[i] < limit]
        whole, left = sum([weights[i] for i in candidates]), spare
        for i in candidates:
            addition = min(limit - given[i], max(1, left * weights[i] // whole), spare)
            given[i] = given[i] + addition
            spare = spare - addition
    return np.array(given)


def centred(stream_key, shape, spread, bound, cuts=(), held_as=jnp.bfloat16):
    factor_of = steps_of(stream_key, shape, cuts, -0.22, 0.18) if cuts else 1.0
    values = jax.random.normal(stream_key, shape, jnp.float32) * spread * factor_of
    return jnp.minimum(jnp.maximum(values, -bound), bound).astype(held_as)


def setup_inputs(seed: int = 0) -> dict:
    key_list = jax.random.split(jax.random.key(seed), 6)
    cotangent = centred(key_list[0], (TOKENS, D), 1.0, 6.0, ((0, 256),))
    saved_gate_up = centred(key_list[1], (TOKENS, TOP, 2 * FF), 1.0, 6.0, ((0, 256),))
    route_ids_keys = jax.random.split(jax.random.fold_in(key_list[2], 1), TOKENS // TOK_DEV)
    route_ids_turns = jax.random.permutation(jax.random.fold_in(key_list[2], 3), TOKENS // TOK_DEV)
    route_ids = jax.vmap(lambda own, number: assign_block(jax.random.fold_in(key_list[2], 2), own, number, TOK_DEV, EXPERTS, TOP, CAP, 2))(route_ids_keys, route_ids_turns).reshape((TOKENS, TOP))
    route_weights = jnp.clip(jnp.exp(math.log(1.0) - 2.9957323 * jax.random.uniform(key_list[3], (TOKENS, TOP), jnp.float32) ** steps_of(key_list[3], (TOKENS, TOP), ((0, 256),), -0.2, 0.2)), 0.05, 1.0)
    w_down = centred(key_list[4], (EXPERTS, FF, D), FF ** -0.5, 0.21875, ((0, 16), (1, 16)))
    return {"cotangent": cotangent, "saved_gate_up": saved_gate_up, "route_ids": route_ids, "route_weights": route_weights, "w_down": w_down}


def slot_positions(flat_ids, experts, capacity):
    onehot = (flat_ids[:, None] == jnp.arange(experts, dtype=jnp.int32)[None, :]).astype(jnp.int32)
    before = jnp.cumsum(onehot, axis=0) - onehot
    slot = jnp.sum(before * onehot, axis=1).astype(jnp.int32)
    return (flat_ids * capacity + slot).astype(jnp.int32)


def reference(cotangent, saved_gate_up, route_ids, route_weights, w_down):
    devices = N_DP * N_EXPERT
    routes = TOK_DEV * TOP
    total = TOKENS * TOP
    gate = saved_gate_up[:, :, :FF].astype(jnp.float32)
    up = saved_gate_up[:, :, FF:].astype(jnp.float32)
    sig = jax.nn.sigmoid(gate)
    act = gate * sig
    hidden = (act * up).astype(jnp.bfloat16)
    weights = route_weights[:, :, None]
    scaled = (weights * hidden.astype(jnp.float32)).astype(jnp.bfloat16)
    ids = route_ids.reshape(devices, routes)
    position = jax.vmap(lambda row: slot_positions(row, EXPERTS, CAP))(ids)
    global_index = (jnp.arange(devices, dtype=jnp.int32)[:, None] * routes
                    + jnp.arange(routes, dtype=jnp.int32)[None, :]).astype(jnp.int32)
    table = jnp.full((devices, EXPERTS * CAP), total, jnp.int32)
    table = table.at[jnp.arange(devices, dtype=jnp.int32)[:, None], position].set(global_index)
    table = table.reshape(devices, EXPERTS, CAP).transpose(1, 0, 2).reshape(EXPERTS, devices * CAP)
    dy_ext = jnp.concatenate([cotangent, jnp.zeros((1, D), cotangent.dtype)], 0)
    h_ext = jnp.concatenate([scaled.reshape(total, FF), jnp.zeros((1, FF), scaled.dtype)], 0)

    def per_expert(carry, inputs):
        index, weight = inputs
        dy_rows = dy_ext[index // TOP]
        h_rows = h_ext[index]
        grads = jnp.dot(dy_rows, weight.T, preferred_element_type=jnp.float32).astype(jnp.bfloat16)
        carry = carry.at[index].set(grads)
        parts = jnp.einsum("pnf,pnd->pfd",
                           h_rows.reshape(N_DP, N_EXPERT * CAP, FF).astype(jnp.float32),
                           dy_rows.reshape(N_DP, N_EXPERT * CAP, D).astype(jnp.float32))
        parts = lax.optimization_barrier(parts.astype(jnp.bfloat16)).astype(jnp.float32)
        return carry, jnp.sum(parts, 0)

    init = jnp.zeros((total + 1, FF), jnp.bfloat16)
    q_all, grad_down = lax.scan(per_expert, init, (table, w_down))
    qf = q_all[:total].reshape(TOKENS, TOP, FF).astype(jnp.float32)
    route_grad = jnp.sum(qf * hidden.astype(jnp.float32), -1)
    d_hidden = weights * qf
    d_gate = d_hidden * up * sig * (1.0 + gate * (1.0 - sig))
    d_up = d_hidden * act
    grad_gate_up = jnp.concatenate([d_gate, d_up], -1).astype(jnp.bfloat16)
    return grad_gate_up, route_grad, grad_down
```

```python
import jax
import jax.numpy as jnp
from jax import lax
from jax.sharding import PartitionSpec as P


def slot_counts(ids, experts):
    routes = ids.shape[-1]
    onehot = (ids[..., None] == jnp.arange(experts, dtype=jnp.int32)).astype(jnp.bfloat16)
    lower = (jnp.arange(routes)[:, None] > jnp.arange(routes)[None, :]).astype(jnp.bfloat16)
    before = jnp.einsum("rq,...qe->...re", lower, onehot, preferred_element_type=jnp.float32)
    return jnp.sum(before * onehot.astype(jnp.float32), axis=-1).astype(jnp.int32)


def local(cotangent, saved_gate_up, route_ids, route_weights, w_down):
    tokens, top = route_ids.shape
    width = cotangent.shape[1]
    hidden_units = saved_gate_up.shape[2] // 2
    owners = lax.axis_size("expert")
    replicas = lax.axis_size("dp")
    me = lax.axis_index("expert")
    local_experts = w_down.shape[0]
    experts = local_experts * owners
    capacity = min(tokens, 2 * tokens * top // experts)
    routes = tokens * top

    cot_group = lax.all_gather(cotangent, "expert", axis=0, tiled=True)
    ids_group = lax.all_gather(route_ids.reshape(1, routes), "expert", axis=0, tiled=True)
    full_down = lax.all_gather(w_down, "dp", axis=1, tiled=True)

    gate = saved_gate_up[:, :, :hidden_units].astype(jnp.float32)
    up = saved_gate_up[:, :, hidden_units:].astype(jnp.float32)
    sig = jax.nn.sigmoid(gate)
    act = gate * sig
    hidden = (act * up).astype(jnp.bfloat16)
    weights = route_weights[:, :, None]
    scaled = (weights * hidden.astype(jnp.float32)).astype(jnp.bfloat16)

    flat_ids = route_ids.reshape(routes)
    slot = slot_counts(flat_ids, experts)
    position = flat_ids * capacity + slot
    slot_ids = jnp.arange(experts * capacity, dtype=jnp.int32)
    match = position[None, :] == slot_ids[:, None]
    route_of_slot = jnp.sum(jnp.where(match, jnp.arange(routes, dtype=jnp.int32)[None, :], 0), axis=1)
    filled = jnp.any(match, axis=1)
    h_rows = jnp.where(filled[:, None], scaled.reshape(routes, hidden_units)[route_of_slot], jnp.zeros((), jnp.bfloat16))
    h_send = h_rows.reshape(owners, local_experts, capacity, hidden_units)

    slot_all = slot_counts(ids_group, experts)
    mine = me * local_experts + jnp.arange(local_experts, dtype=jnp.int32)
    pos_all = ids_group * capacity + slot_all
    want = (mine[:, None] * capacity + jnp.arange(capacity, dtype=jnp.int32)[None, :]).reshape(-1)
    hit = pos_all[:, None, :] == want[None, :, None]
    token_of = jnp.sum(jnp.where(hit, (jnp.arange(routes, dtype=jnp.int32) // top)[None, None, :], 0), axis=2)
    rows = (jnp.arange(owners, dtype=jnp.int32)[:, None] * tokens + token_of).reshape(owners, local_experts, capacity)
    rows = jnp.transpose(rows, (1, 0, 2)).reshape(local_experts, owners * capacity)
    dy_recv = cot_group[rows]

    h_recv = lax.all_to_all(h_send, "expert", split_axis=0, concat_axis=2, tiled=True)[0]
    grads = jnp.einsum(
        "jsd,jfd->jsf", dy_recv, full_down, preferred_element_type=jnp.float32
    ).astype(jnp.bfloat16)
    back = lax.all_to_all(
        grads.reshape(1, local_experts, owners * capacity, hidden_units),
        "expert",
        split_axis=2,
        concat_axis=0,
        tiled=True,
    )
    parts = []
    for j in range(local_experts):
        part = jnp.einsum(
            "sf,sd->fd", h_recv[j], dy_recv[j], preferred_element_type=jnp.float32
        ).astype(jnp.bfloat16)
        parts.append(lax.psum_scatter(part, "dp", scatter_dimension=0, tiled=True).astype(jnp.float32))
    grad_down = jnp.stack(parts)
    returned_rows = back.reshape(experts * capacity, hidden_units)[position]
    qf = returned_rows.reshape(tokens, top, hidden_units).astype(jnp.float32)
    route_grad = jnp.sum(qf * hidden.astype(jnp.float32), -1)
    d_hidden = weights * qf
    d_gate = d_hidden * up * sig * (1.0 + gate * (1.0 - sig))
    d_up = d_hidden * act
    grad_gate_up = jnp.concatenate([d_gate, d_up], -1).astype(jnp.bfloat16)
    return (grad_gate_up, route_grad, grad_down)


def solution(mesh):
    return jax.shard_map(
        local,
        mesh=mesh,
        in_specs=(
            P(("dp", "expert"), None),
            P(("dp", "expert"), None, None),
            P(("dp", "expert"), None),
            P(("dp", "expert"), None),
            P("expert", "dp", None),
        ),
        out_specs=(
            P(("dp", "expert"), None, None),
            P(("dp", "expert"), None),
            P("expert", "dp", None),
        ),
        check_vma=False,
    )
```

```python
import jax
import jax.numpy as jnp
from jax import lax
from jax.sharding import PartitionSpec as P


def slot_counts(ids, experts):
    routes = ids.shape[-1]
    onehot = (ids[..., None] == jnp.arange(experts, dtype=jnp.int32)).astype(jnp.bfloat16)
    lower = (jnp.arange(routes)[:, None] > jnp.arange(routes)[None, :]).astype(jnp.bfloat16)
    before = jnp.einsum("rq,...qe->...re", lower, onehot, preferred_element_type=jnp.float32)
    return jnp.sum(before * onehot.astype(jnp.float32), axis=-1).astype(jnp.int32)


def local(cotangent, saved_gate_up, route_ids, route_weights, w_down):
    tokens, top = route_ids.shape
    width = cotangent.shape[1]
    hidden_units = saved_gate_up.shape[2] // 2
    owners = lax.axis_size("expert")
    replicas = lax.axis_size("dp")
    me = lax.axis_index("expert")
    local_experts = w_down.shape[0]
    experts = local_experts * owners
    capacity = min(tokens, 2 * tokens * top // experts)
    routes = tokens * top

    cot_group = lax.all_gather(cotangent, "expert", axis=0, tiled=True)
    ids_group = lax.all_gather(route_ids.reshape(1, routes), "expert", axis=0, tiled=True)
    full_down = lax.all_gather(w_down, "dp", axis=1, tiled=True)

    gate = saved_gate_up[:, :, :hidden_units].astype(jnp.float32)
    up = saved_gate_up[:, :, hidden_units:].astype(jnp.float32)
    sig = jax.nn.sigmoid(gate)
    act = gate * sig
    hidden = (act * up).astype(jnp.bfloat16)
    weights = route_weights[:, :, None]
    scaled = (weights * hidden.astype(jnp.float32)).astype(jnp.bfloat16)

    flat_ids = route_ids.reshape(routes)
    slot = slot_counts(flat_ids, experts)
    position = flat_ids * capacity + slot
    slot_ids = jnp.arange(experts * capacity, dtype=jnp.int32)
    match = position[None, :] == slot_ids[:, None]
    route_of_slot = jnp.sum(jnp.where(match, jnp.arange(routes, dtype=jnp.int32)[None, :], 0), axis=1)
    filled = jnp.any(match, axis=1)
    h_rows = jnp.where(filled[:, None], scaled.reshape(routes, hidden_units)[route_of_slot], jnp.zeros((), jnp.bfloat16))
    h_send = h_rows.reshape(owners, local_experts, capacity, hidden_units)

    slot_all = slot_counts(ids_group, experts)
    mine = me * local_experts + jnp.arange(local_experts, dtype=jnp.int32)
    pos_all = ids_group * capacity + slot_all
    want = (mine[:, None] * capacity + jnp.arange(capacity, dtype=jnp.int32)[None, :]).reshape(-1)
    hit = pos_all[:, None, :] == want[None, :, None]
    token_of = jnp.sum(jnp.where(hit, (jnp.arange(routes, dtype=jnp.int32) // top)[None, None, :], 0), axis=2)
    rows = (jnp.arange(owners, dtype=jnp.int32)[:, None] * tokens + token_of).reshape(owners, local_experts, capacity)
    rows = jnp.transpose(rows, (1, 0, 2)).reshape(local_experts, owners * capacity)
    h_recv = lax.all_to_all(h_send, "expert", split_axis=0, concat_axis=2, tiled=True)[0]
    h_recv, cot_group = lax.optimization_barrier((h_recv, cot_group))
    dy_recv = cot_group[rows]

    grads = jnp.einsum(
        "jsd,jfd->jsf", dy_recv, full_down, preferred_element_type=jnp.float32
    ).astype(jnp.bfloat16)
    back = lax.all_to_all(
        grads.reshape(1, local_experts, owners * capacity, hidden_units),
        "expert",
        split_axis=2,
        concat_axis=0,
        tiled=True,
    )
    parts = []
    for j in range(local_experts):
        part = jnp.einsum(
            "sf,sd->fd", h_recv[j], dy_recv[j], preferred_element_type=jnp.float32
        ).astype(jnp.bfloat16)
        parts.append(part.reshape(replicas, hidden_units // replicas, width))
    summed = lax.psum_scatter(jnp.stack(parts, axis=1), "dp", scatter_dimension=0, tiled=True)
    grad_down = summed[0].astype(jnp.float32)
    returned_rows = back.reshape(experts * capacity, hidden_units)[position]
    qf = returned_rows.reshape(tokens, top, hidden_units).astype(jnp.float32)
    route_grad = jnp.sum(qf * hidden.astype(jnp.float32), -1)
    d_hidden = weights * qf
    d_gate = d_hidden * up * sig * (1.0 + gate * (1.0 - sig))
    d_up = d_hidden * act
    grad_gate_up = jnp.concatenate([d_gate, d_up], -1).astype(jnp.bfloat16)
    return (grad_gate_up, route_grad, grad_down)


def solution(mesh):
    return jax.shard_map(
        local,
        mesh=mesh,
        in_specs=(
            P(("dp", "expert"), None),
            P(("dp", "expert"), None, None),
            P(("dp", "expert"), None),
            P(("dp", "expert"), None),
            P("expert", "dp", None),
        ),
        out_specs=(
            P(("dp", "expert"), None, None),
            P(("dp", "expert"), None),
            P("expert", "dp", None),
        ),
        check_vma=False,
    )
```

```python
import jax
import jax.numpy as jnp
from jax import lax
from jax.experimental import pallas as pl
from jax.experimental.pallas import tpu as pltpu
from jax.sharding import PartitionSpec as P

MESH = pl.DeviceIdType.MESH


def ring_dp(pos, replicas):
    pos = lax.rem(pos + 2 * replicas, replicas)
    z = pos // 2
    core = lax.rem(pos, 2)
    core = jnp.where(lax.rem(z, 2) == 0, core, 1 - core)
    return z * 2 + core


def ring_pos(dp):
    z = dp // 2
    core = lax.rem(dp, 2)
    return z * 2 + jnp.where(lax.rem(z, 2) == 0, core, 1 - core)


def gather_kernel(replicas, w_ref, o_ref, own_sem, send_sem, recv_sem):
    me = lax.axis_index("dp")
    col = lax.axis_index("expert")
    pos = ring_pos(me)
    right = ring_dp(pos + 1, replicas)
    left = ring_dp(pos - 1, replicas)

    barrier = pltpu.get_barrier_semaphore()
    for neighbour in (left, right):
        pl.semaphore_signal(barrier, inc=1, device_id=(neighbour, col), device_id_type=MESH)
    pl.semaphore_wait(barrier, 2)

    own = pltpu.make_async_copy(w_ref, o_ref.at[me], own_sem)
    own.start()
    for step in range(replicas - 1):
        copies = []
        for j, (target, origin) in enumerate(((right, pos - step), (left, pos + step))):
            block = ring_dp(origin, replicas)
            src = w_ref.at[j] if step == 0 else o_ref.at[block, j]
            copy = pltpu.make_async_remote_copy(
                src_ref=src,
                dst_ref=o_ref.at[block, j],
                send_sem=send_sem.at[j, step],
                recv_sem=recv_sem.at[j, step],
                device_id=(target, col),
                device_id_type=MESH,
            )
            copy.start()
            copies.append(copy)
        for copy in copies:
            copy.wait()
    own.wait()


def gather_down(w_down, replicas):
    local_experts, rows, width = w_down.shape
    return pl.pallas_call(
        lambda *refs: gather_kernel(replicas, *refs),
        out_shape=jax.ShapeDtypeStruct((replicas, local_experts, rows, width), w_down.dtype),
        in_specs=[pl.BlockSpec(memory_space=pl.ANY)],
        out_specs=pl.BlockSpec(memory_space=pl.ANY),
        scratch_shapes=[
            pltpu.SemaphoreType.DMA(()),
            pltpu.SemaphoreType.DMA((2, replicas - 1)),
            pltpu.SemaphoreType.DMA((2, replicas - 1)),
        ],
        compiler_params=pltpu.CompilerParams(collective_id=0, has_side_effects=True),
        cost_estimate=pl.CostEstimate(
            flops=0, bytes_accessed=2 * replicas * w_down.size * 2, transcendentals=0
        ),
    )(w_down)


def slot_counts(ids, experts):
    routes = ids.shape[-1]
    onehot = (ids[..., None] == jnp.arange(experts, dtype=jnp.int32)).astype(jnp.bfloat16)
    lower = (jnp.arange(routes)[:, None] > jnp.arange(routes)[None, :]).astype(jnp.bfloat16)
    before = jnp.einsum("rq,...qe->...re", lower, onehot, preferred_element_type=jnp.float32)
    return jnp.sum(before * onehot.astype(jnp.float32), axis=-1).astype(jnp.int32)


def local(cotangent, saved_gate_up, route_ids, route_weights, w_down):
    tokens, top = route_ids.shape
    width = cotangent.shape[1]
    hidden_units = saved_gate_up.shape[2] // 2
    owners = lax.axis_size("expert")
    replicas = lax.axis_size("dp")
    me = lax.axis_index("expert")
    local_experts = w_down.shape[0]
    experts = local_experts * owners
    capacity = min(tokens, 2 * tokens * top // experts)
    routes = tokens * top

    cot_group = lax.all_gather(cotangent, "expert", axis=0, tiled=True)
    ids_group = lax.all_gather(route_ids.reshape(1, routes), "expert", axis=0, tiled=True)
    full_down = gather_down(w_down, replicas)

    gate = saved_gate_up[:, :, :hidden_units].astype(jnp.float32)
    up = saved_gate_up[:, :, hidden_units:].astype(jnp.float32)
    sig = jax.nn.sigmoid(gate)
    act = gate * sig
    hidden = (act * up).astype(jnp.bfloat16)
    weights = route_weights[:, :, None]
    scaled = (weights * hidden.astype(jnp.float32)).astype(jnp.bfloat16)

    flat_ids = route_ids.reshape(routes)
    slot = slot_counts(flat_ids, experts)
    position = flat_ids * capacity + slot
    slot_ids = jnp.arange(experts * capacity, dtype=jnp.int32)
    match = position[None, :] == slot_ids[:, None]
    route_of_slot = jnp.sum(jnp.where(match, jnp.arange(routes, dtype=jnp.int32)[None, :], 0), axis=1)
    filled = jnp.any(match, axis=1)
    h_rows = jnp.where(filled[:, None], scaled.reshape(routes, hidden_units)[route_of_slot], jnp.zeros((), jnp.bfloat16))
    h_send = h_rows.reshape(owners, local_experts, capacity, hidden_units)

    slot_all = slot_counts(ids_group, experts)
    mine = me * local_experts + jnp.arange(local_experts, dtype=jnp.int32)
    pos_all = ids_group * capacity + slot_all
    want = (mine[:, None] * capacity + jnp.arange(capacity, dtype=jnp.int32)[None, :]).reshape(-1)
    hit = pos_all[:, None, :] == want[None, :, None]
    token_of = jnp.sum(jnp.where(hit, (jnp.arange(routes, dtype=jnp.int32) // top)[None, None, :], 0), axis=2)
    rows = (jnp.arange(owners, dtype=jnp.int32)[:, None] * tokens + token_of).reshape(owners, local_experts, capacity)
    rows = jnp.transpose(rows, (1, 0, 2)).reshape(local_experts, owners * capacity)
    full_down, h_send = lax.optimization_barrier((full_down, h_send))
    h_recv = lax.all_to_all(h_send, "expert", split_axis=0, concat_axis=2, tiled=True)[0]
    h_recv, cot_group = lax.optimization_barrier((h_recv, cot_group))
    dy_recv = cot_group[rows]

    grads = jnp.einsum(
        "jsd,qjid->jsqi", dy_recv, full_down, preferred_element_type=jnp.float32
    ).astype(jnp.bfloat16).reshape(local_experts, owners * capacity, hidden_units)
    back = lax.all_to_all(
        grads.reshape(1, local_experts, owners * capacity, hidden_units),
        "expert",
        split_axis=2,
        concat_axis=0,
        tiled=True,
    )
    parts = []
    for j in range(local_experts):
        part = jnp.einsum(
            "sf,sd->fd", h_recv[j], dy_recv[j], preferred_element_type=jnp.float32
        ).astype(jnp.bfloat16)
        parts.append(part.reshape(replicas, hidden_units // replicas, width))
    summed = lax.psum_scatter(jnp.stack(parts, axis=1), "dp", scatter_dimension=0, tiled=True)
    grad_down = summed[0].astype(jnp.float32)
    returned_rows = back.reshape(experts * capacity, hidden_units)[position]
    qf = returned_rows.reshape(tokens, top, hidden_units).astype(jnp.float32)
    route_grad = jnp.sum(qf * hidden.astype(jnp.float32), -1)
    d_hidden = weights * qf
    d_gate = d_hidden * up * sig * (1.0 + gate * (1.0 - sig))
    d_up = d_hidden * act
    grad_gate_up = jnp.concatenate([d_gate, d_up], -1).astype(jnp.bfloat16)
    return (grad_gate_up, route_grad, grad_down)


def solution(mesh):
    return jax.shard_map(
        local,
        mesh=mesh,
        in_specs=(
            P(("dp", "expert"), None),
            P(("dp", "expert"), None, None),
            P(("dp", "expert"), None),
            P(("dp", "expert"), None),
            P("expert", "dp", None),
        ),
        out_specs=(
            P(("dp", "expert"), None, None),
            P(("dp", "expert"), None),
            P("expert", "dp", None),
        ),
        check_vma=False,
    )
```

```python
import jax
import jax.numpy as jnp
from jax import lax
from jax.experimental import pallas as pl
from jax.experimental.pallas import tpu as pltpu
from jax.sharding import PartitionSpec as P

MESH = pl.DeviceIdType.MESH


def ring_dp(pos, replicas):
    pos = lax.rem(pos + 2 * replicas, replicas)
    z = pos // 2
    core = lax.rem(pos, 2)
    core = jnp.where(lax.rem(z, 2) == 0, core, 1 - core)
    return z * 2 + core


def ring_pos(dp):
    z = dp // 2
    core = lax.rem(dp, 2)
    return z * 2 + jnp.where(lax.rem(z, 2) == 0, core, 1 - core)


def gather_kernel(replicas, pieces, w_ref, o_ref, own_sem, send_sem, recv_sem):
    me = lax.axis_index("dp")
    col = lax.axis_index("expert")
    pos = ring_pos(me)
    right = ring_dp(pos + 1, replicas)
    left = ring_dp(pos - 1, replicas)
    cols = w_ref.shape[2] // pieces

    barrier = pltpu.get_barrier_semaphore()
    for neighbour in (left, right):
        pl.semaphore_signal(barrier, inc=1, device_id=(neighbour, col), device_id_type=MESH)
    pl.semaphore_wait(barrier, 2)

    own = pltpu.make_async_copy(w_ref, o_ref.at[me], own_sem)
    own.start()
    hops = (replicas // 2, replicas - 1 - replicas // 2)
    for step in range(hops[0]):
        copies = []
        for way, (target, sign) in enumerate(((right, -1), (left, 1))):
            if step >= hops[way]:
                continue
            block = ring_dp(pos + sign * step, replicas)
            for piece in range(pieces):
                part = pl.ds(piece * cols, cols)
                src = w_ref.at[:, :, part] if step == 0 else o_ref.at[block, :, :, part]
                copy = pltpu.make_async_remote_copy(
                    src_ref=src,
                    dst_ref=o_ref.at[block, :, :, part],
                    send_sem=send_sem.at[way, step, piece],
                    recv_sem=recv_sem.at[way, step, piece],
                    device_id=(target, col),
                    device_id_type=MESH,
                )
                copy.start()
                copies.append(copy)
        for copy in copies:
            copy.wait()
    own.wait()


def gather_down(w_down, replicas, pieces=4):
    local_experts, rows, width = w_down.shape
    return pl.pallas_call(
        lambda *refs: gather_kernel(replicas, pieces, *refs),
        out_shape=jax.ShapeDtypeStruct((replicas, local_experts, rows, width), w_down.dtype),
        in_specs=[pl.BlockSpec(memory_space=pl.ANY)],
        out_specs=pl.BlockSpec(memory_space=pl.ANY),
        scratch_shapes=[
            pltpu.SemaphoreType.DMA(()),
            pltpu.SemaphoreType.DMA((2, replicas // 2, pieces)),
            pltpu.SemaphoreType.DMA((2, replicas // 2, pieces)),
        ],
        compiler_params=pltpu.CompilerParams(collective_id=0, has_side_effects=True),
        cost_estimate=pl.CostEstimate(
            flops=0, bytes_accessed=2 * replicas * w_down.size * 2, transcendentals=0
        ),
    )(w_down)


def slot_counts(ids, experts):
    routes = ids.shape[-1]
    onehot = (ids[..., None] == jnp.arange(experts, dtype=jnp.int32)).astype(jnp.bfloat16)
    lower = (jnp.arange(routes)[:, None] > jnp.arange(routes)[None, :]).astype(jnp.bfloat16)
    before = jnp.einsum("rq,...qe->...re", lower, onehot, preferred_element_type=jnp.float32)
    return jnp.sum(before * onehot.astype(jnp.float32), axis=-1).astype(jnp.int32)


def local(cotangent, saved_gate_up, route_ids, route_weights, w_down):
    tokens, top = route_ids.shape
    width = cotangent.shape[1]
    hidden_units = saved_gate_up.shape[2] // 2
    owners = lax.axis_size("expert")
    replicas = lax.axis_size("dp")
    me = lax.axis_index("expert")
    local_experts = w_down.shape[0]
    experts = local_experts * owners
    capacity = min(tokens, 2 * tokens * top // experts)
    routes = tokens * top

    lanes = 128
    ids_cols = jnp.pad(route_ids.astype(jnp.bfloat16), ((0, 0), (0, lanes - top)))
    cot_ext = lax.all_gather(
        jnp.concatenate([cotangent, ids_cols], axis=1), "expert", axis=0, tiled=True
    )
    ids_group = cot_ext[:, width:width + top].astype(jnp.int32).reshape(owners, routes)
    cot_group = cot_ext[:, :width]
    full_down = gather_down(w_down, replicas)

    gate = saved_gate_up[:, :, :hidden_units].astype(jnp.float32)
    up = saved_gate_up[:, :, hidden_units:].astype(jnp.float32)
    sig = jax.nn.sigmoid(gate)
    act = gate * sig
    hidden = (act * up).astype(jnp.bfloat16)
    weights = route_weights[:, :, None]
    scaled = (weights * hidden.astype(jnp.float32)).astype(jnp.bfloat16)

    flat_ids = route_ids.reshape(routes)
    slot = slot_counts(flat_ids, experts)
    position = flat_ids * capacity + slot
    slot_ids = jnp.arange(experts * capacity, dtype=jnp.int32)
    match = position[None, :] == slot_ids[:, None]
    route_of_slot = jnp.sum(jnp.where(match, jnp.arange(routes, dtype=jnp.int32)[None, :], 0), axis=1)
    filled = jnp.any(match, axis=1)
    h_rows = jnp.where(filled[:, None], scaled.reshape(routes, hidden_units)[route_of_slot], jnp.zeros((), jnp.bfloat16))
    h_send = h_rows.reshape(owners, local_experts, capacity, hidden_units)

    slot_all = slot_counts(ids_group, experts)
    mine = me * local_experts + jnp.arange(local_experts, dtype=jnp.int32)
    pos_all = ids_group * capacity + slot_all
    want = (mine[:, None] * capacity + jnp.arange(capacity, dtype=jnp.int32)[None, :]).reshape(-1)
    hit = pos_all[:, None, :] == want[None, :, None]
    token_of = jnp.sum(jnp.where(hit, (jnp.arange(routes, dtype=jnp.int32) // top)[None, None, :], 0), axis=2)
    rows = (jnp.arange(owners, dtype=jnp.int32)[:, None] * tokens + token_of).reshape(owners, local_experts, capacity)
    rows = jnp.transpose(rows, (1, 0, 2)).reshape(local_experts, owners * capacity)
    full_down, h_send = lax.optimization_barrier((full_down, h_send))
    h_recv = lax.all_to_all(h_send, "expert", split_axis=0, concat_axis=2, tiled=True)[0]
    h_recv, cot_group = lax.optimization_barrier((h_recv, cot_group))
    dy_recv = cot_group[rows]

    grads = jnp.einsum(
        "jsd,qjid->jsqi", dy_recv, full_down, preferred_element_type=jnp.float32
    ).astype(jnp.bfloat16).reshape(local_experts, owners * capacity, hidden_units)
    back = lax.all_to_all(
        grads.reshape(1, local_experts, owners * capacity, hidden_units),
        "expert",
        split_axis=2,
        concat_axis=0,
        tiled=True,
    )
    parts = []
    for j in range(local_experts):
        part = jnp.einsum(
            "sf,sd->fd", h_recv[j], dy_recv[j], preferred_element_type=jnp.float32
        ).astype(jnp.bfloat16)
        parts.append(part.reshape(replicas, hidden_units // replicas, width))
    summed = lax.psum_scatter(jnp.stack(parts, axis=1), "dp", scatter_dimension=0, tiled=True)
    grad_down = summed[0].astype(jnp.float32)
    returned_rows = back.reshape(experts * capacity, hidden_units)[position]
    qf = returned_rows.reshape(tokens, top, hidden_units).astype(jnp.float32)
    route_grad = jnp.sum(qf * hidden.astype(jnp.float32), -1)
    d_hidden = weights * qf
    d_gate = d_hidden * up * sig * (1.0 + gate * (1.0 - sig))
    d_up = d_hidden * act
    grad_gate_up = jnp.concatenate([d_gate, d_up], -1).astype(jnp.bfloat16)
    return (grad_gate_up, route_grad, grad_down)


def solution(mesh):
    return jax.shard_map(
        local,
        mesh=mesh,
        in_specs=(
            P(("dp", "expert"), None),
            P(("dp", "expert"), None, None),
            P(("dp", "expert"), None),
            P(("dp", "expert"), None),
            P("expert", "dp", None),
        ),
        out_specs=(
            P(("dp", "expert"), None, None),
            P(("dp", "expert"), None),
            P("expert", "dp", None),
        ),
        check_vma=False,
    )
```

```python
import jax
import jax.numpy as jnp
from jax import lax
from jax.experimental import pallas as pl
from jax.experimental.pallas import tpu as pltpu
from jax.sharding import PartitionSpec as P

MESH = pl.DeviceIdType.MESH


def ring_dp(pos, replicas):
    pos = lax.rem(pos + 2 * replicas, replicas)
    z = pos // 2
    core = lax.rem(pos, 2)
    core = jnp.where(lax.rem(z, 2) == 0, core, 1 - core)
    return z * 2 + core


def ring_pos(dp):
    z = dp // 2
    core = lax.rem(dp, 2)
    return z * 2 + jnp.where(lax.rem(z, 2) == 0, core, 1 - core)


def exchange_kernel(replicas, owners, pieces, w_ref, h_ref, o_ref, g_ref, sems, send_sem, recv_sem,
                    h_send_sem, h_recv_sem):
    me = lax.axis_index("dp")
    col = lax.axis_index("expert")
    pos = ring_pos(me)
    right = ring_dp(pos + 1, replicas)
    left = ring_dp(pos - 1, replicas)
    cols = w_ref.shape[2] // pieces

    barrier = pltpu.get_barrier_semaphore()
    for neighbour in (left, right):
        pl.semaphore_signal(barrier, inc=1, device_id=(neighbour, col), device_id_type=MESH)
    for peer in range(owners - 1):
        other = lax.rem(col + 1 + peer, owners)
        pl.semaphore_signal(barrier, inc=1, device_id=(me, other), device_id_type=MESH)
    pl.semaphore_wait(barrier, 2 + owners - 1)

    own = pltpu.make_async_copy(w_ref, o_ref.at[me], sems.at[0])
    own.start()
    own_h = pltpu.make_async_copy(h_ref.at[col], g_ref.at[col], sems.at[1])
    own_h.start()
    outgoing = []
    for peer in range(owners - 1):
        other = lax.rem(col + 1 + peer, owners)
        copy = pltpu.make_async_remote_copy(
            src_ref=h_ref.at[other],
            dst_ref=g_ref.at[col],
            send_sem=h_send_sem.at[other],
            recv_sem=h_recv_sem.at[col],
            device_id=(me, other),
            device_id_type=MESH,
        )
        copy.start()
        outgoing.append(copy)

    hops = (replicas // 2, replicas - 1 - replicas // 2)
    for step in range(hops[0]):
        copies = []
        for way, (target, sign) in enumerate(((right, -1), (left, 1))):
            if step >= hops[way]:
                continue
            block = ring_dp(pos + sign * step, replicas)
            for piece in range(pieces):
                part = pl.ds(piece * cols, cols)
                src = w_ref.at[:, :, part] if step == 0 else o_ref.at[block, :, :, part]
                copy = pltpu.make_async_remote_copy(
                    src_ref=src,
                    dst_ref=o_ref.at[block, :, :, part],
                    send_sem=send_sem.at[way, step, piece],
                    recv_sem=recv_sem.at[way, step, piece],
                    device_id=(target, col),
                    device_id_type=MESH,
                )
                copy.start()
                copies.append(copy)
        for copy in copies:
            copy.wait()

    for copy in outgoing:
        copy.wait_send()
    for peer in range(owners - 1):
        source = lax.rem(col + 1 + peer, owners)
        incoming = pltpu.make_async_remote_copy(
            src_ref=h_ref.at[source],
            dst_ref=g_ref.at[source],
            send_sem=h_send_sem.at[source],
            recv_sem=h_recv_sem.at[source],
            device_id=(me, source),
            device_id_type=MESH,
        )
        incoming.wait_recv()
    own.wait()
    own_h.wait()


def exchange(w_down, h_send, replicas, owners, pieces=4):
    return pl.pallas_call(
        lambda *refs: exchange_kernel(replicas, owners, pieces, *refs),
        out_shape=(
            jax.ShapeDtypeStruct((replicas,) + w_down.shape, w_down.dtype),
            jax.ShapeDtypeStruct(h_send.shape, h_send.dtype),
        ),
        in_specs=[pl.BlockSpec(memory_space=pl.ANY)] * 2,
        out_specs=(pl.BlockSpec(memory_space=pl.ANY), pl.BlockSpec(memory_space=pl.ANY)),
        scratch_shapes=[
            pltpu.SemaphoreType.DMA((2,)),
            pltpu.SemaphoreType.DMA((2, replicas // 2, pieces)),
            pltpu.SemaphoreType.DMA((2, replicas // 2, pieces)),
            pltpu.SemaphoreType.DMA((owners,)),
            pltpu.SemaphoreType.DMA((owners,)),
        ],
        compiler_params=pltpu.CompilerParams(collective_id=0, has_side_effects=True),
        cost_estimate=pl.CostEstimate(
            flops=0,
            bytes_accessed=2 * replicas * w_down.size * 2 + 2 * h_send.size * 2,
            transcendentals=0,
        ),
    )(w_down, h_send)


def slot_counts(ids, experts):
    routes = ids.shape[-1]
    onehot = (ids[..., None] == jnp.arange(experts, dtype=jnp.int32)).astype(jnp.bfloat16)
    lower = (jnp.arange(routes)[:, None] > jnp.arange(routes)[None, :]).astype(jnp.bfloat16)
    before = jnp.einsum("rq,...qe->...re", lower, onehot, preferred_element_type=jnp.float32)
    return jnp.sum(before * onehot.astype(jnp.float32), axis=-1).astype(jnp.int32)


def local(cotangent, saved_gate_up, route_ids, route_weights, w_down):
    tokens, top = route_ids.shape
    width = cotangent.shape[1]
    hidden_units = saved_gate_up.shape[2] // 2
    owners = lax.axis_size("expert")
    replicas = lax.axis_size("dp")
    me = lax.axis_index("expert")
    local_experts = w_down.shape[0]
    experts = local_experts * owners
    capacity = min(tokens, 2 * tokens * top // experts)
    routes = tokens * top

    lanes = 128
    ids_cols = jnp.pad(route_ids.astype(jnp.bfloat16), ((0, 0), (0, lanes - top)))
    cot_ext = lax.all_gather(
        jnp.concatenate([cotangent, ids_cols], axis=1), "expert", axis=0, tiled=True
    )
    ids_group = cot_ext[:, width:width + top].astype(jnp.int32).reshape(owners, routes)
    cot_group = cot_ext[:, :width]

    gate = saved_gate_up[:, :, :hidden_units].astype(jnp.float32)
    up = saved_gate_up[:, :, hidden_units:].astype(jnp.float32)
    sig = jax.nn.sigmoid(gate)
    act = gate * sig
    hidden = (act * up).astype(jnp.bfloat16)
    weights = route_weights[:, :, None]
    scaled = (weights * hidden.astype(jnp.float32)).astype(jnp.bfloat16)

    flat_ids = route_ids.reshape(routes)
    slot = slot_counts(flat_ids, experts)
    position = flat_ids * capacity + slot
    slot_ids = jnp.arange(experts * capacity, dtype=jnp.int32)
    match = position[None, :] == slot_ids[:, None]
    route_of_slot = jnp.sum(jnp.where(match, jnp.arange(routes, dtype=jnp.int32)[None, :], 0), axis=1)
    filled = jnp.any(match, axis=1)
    h_rows = jnp.where(filled[:, None], scaled.reshape(routes, hidden_units)[route_of_slot], jnp.zeros((), jnp.bfloat16))
    h_send = h_rows.reshape(owners, local_experts, capacity, hidden_units)

    slot_all = slot_counts(ids_group, experts)
    mine = me * local_experts + jnp.arange(local_experts, dtype=jnp.int32)
    pos_all = ids_group * capacity + slot_all
    want = (mine[:, None] * capacity + jnp.arange(capacity, dtype=jnp.int32)[None, :]).reshape(-1)
    hit = pos_all[:, None, :] == want[None, :, None]
    token_of = jnp.sum(jnp.where(hit, (jnp.arange(routes, dtype=jnp.int32) // top)[None, None, :], 0), axis=2)
    rows = (jnp.arange(owners, dtype=jnp.int32)[:, None] * tokens + token_of).reshape(owners, local_experts, capacity)
    rows = jnp.transpose(rows, (1, 0, 2)).reshape(local_experts, owners * capacity)
    full_down, h_got = exchange(w_down, h_send, replicas, owners)
    h_recv = jnp.transpose(h_got, (1, 0, 2, 3)).reshape(local_experts, owners * capacity, hidden_units)
    h_recv, cot_group = lax.optimization_barrier((h_recv, cot_group))
    dy_recv = cot_group[rows]

    grads = jnp.einsum(
        "jsd,qjid->jsqi", dy_recv, full_down, preferred_element_type=jnp.float32
    ).astype(jnp.bfloat16).reshape(local_experts, owners * capacity, hidden_units)
    back = lax.all_to_all(
        grads.reshape(1, local_experts, owners * capacity, hidden_units),
        "expert",
        split_axis=2,
        concat_axis=0,
        tiled=True,
    )
    parts = []
    for j in range(local_experts):
        part = jnp.einsum(
            "sf,sd->fd", h_recv[j], dy_recv[j], preferred_element_type=jnp.float32
        ).astype(jnp.bfloat16)
        parts.append(part.reshape(replicas, hidden_units // replicas, width))
    summed = lax.psum_scatter(jnp.stack(parts, axis=1), "dp", scatter_dimension=0, tiled=True)
    grad_down = summed[0].astype(jnp.float32)
    returned_rows = back.reshape(experts * capacity, hidden_units)[position]
    qf = returned_rows.reshape(tokens, top, hidden_units).astype(jnp.float32)
    route_grad = jnp.sum(qf * hidden.astype(jnp.float32), -1)
    d_hidden = weights * qf
    d_gate = d_hidden * up * sig * (1.0 + gate * (1.0 - sig))
    d_up = d_hidden * act
    grad_gate_up = jnp.concatenate([d_gate, d_up], -1).astype(jnp.bfloat16)
    return (grad_gate_up, route_grad, grad_down)


def solution(mesh):
    return jax.shard_map(
        local,
        mesh=mesh,
        in_specs=(
            P(("dp", "expert"), None),
            P(("dp", "expert"), None, None),
            P(("dp", "expert"), None),
            P(("dp", "expert"), None),
            P("expert", "dp", None),
        ),
        out_specs=(
            P(("dp", "expert"), None, None),
            P(("dp", "expert"), None),
            P("expert", "dp", None),
        ),
        check_vma=False,
    )
```

```python
import jax
import jax.numpy as jnp
from jax import lax
from jax.experimental import pallas as pl
from jax.experimental.pallas import tpu as pltpu
from jax.sharding import PartitionSpec as P

MESH = pl.DeviceIdType.MESH


def ring_dp(pos, replicas):
    pos = lax.rem(pos + 2 * replicas, replicas)
    z = pos // 2
    core = lax.rem(pos, 2)
    core = jnp.where(lax.rem(z, 2) == 0, core, 1 - core)
    return z * 2 + core


def ring_pos(dp):
    z = dp // 2
    core = lax.rem(dp, 2)
    return z * 2 + jnp.where(lax.rem(z, 2) == 0, core, 1 - core)


def exchange_kernel(replicas, owners, pieces, w_ref, h_ref, t_ref, o_ref, g_ref, u_ref, sems, send_sem,
                    recv_sem, h_send_sem, h_recv_sem, t_send_sem, t_recv_sem):
    me = lax.axis_index("dp")
    col = lax.axis_index("expert")
    pos = ring_pos(me)
    right = ring_dp(pos + 1, replicas)
    left = ring_dp(pos - 1, replicas)
    cols = w_ref.shape[2] // pieces

    barrier = pltpu.get_barrier_semaphore()
    for neighbour in (left, right):
        pl.semaphore_signal(barrier, inc=1, device_id=(neighbour, col), device_id_type=MESH)
    for peer in range(owners - 1):
        other = lax.rem(col + 1 + peer, owners)
        pl.semaphore_signal(barrier, inc=1, device_id=(me, other), device_id_type=MESH)
    pl.semaphore_wait(barrier, 2 + owners - 1)

    own = pltpu.make_async_copy(w_ref, o_ref.at[:, me], sems.at[0])
    own.start()
    own_h = pltpu.make_async_copy(h_ref.at[col], g_ref.at[col], sems.at[1])
    own_h.start()
    own_t = pltpu.make_async_copy(t_ref.at[col], u_ref.at[col], sems.at[2])
    own_t.start()
    outgoing = []
    for peer in range(owners - 1):
        other = lax.rem(col + 1 + peer, owners)
        for src, dst, ssem, rsem in ((h_ref, g_ref, h_send_sem, h_recv_sem), (t_ref, u_ref, t_send_sem, t_recv_sem)):
            copy = pltpu.make_async_remote_copy(
                src_ref=src.at[other],
                dst_ref=dst.at[col],
                send_sem=ssem.at[other],
                recv_sem=rsem.at[col],
                device_id=(me, other),
                device_id_type=MESH,
            )
            copy.start()
            outgoing.append(copy)

    hops = (replicas // 2, replicas - 1 - replicas // 2)
    for step in range(hops[0]):
        copies = []
        for way, (target, sign) in enumerate(((right, -1), (left, 1))):
            if step >= hops[way]:
                continue
            block = ring_dp(pos + sign * step, replicas)
            for piece in range(pieces):
                part = pl.ds(piece * cols, cols)
                src = w_ref.at[:, :, part] if step == 0 else o_ref.at[:, block, :, part]
                copy = pltpu.make_async_remote_copy(
                    src_ref=src,
                    dst_ref=o_ref.at[:, block, :, part],
                    send_sem=send_sem.at[way, step, piece],
                    recv_sem=recv_sem.at[way, step, piece],
                    device_id=(target, col),
                    device_id_type=MESH,
                )
                copy.start()
                copies.append(copy)
        for copy in copies:
            copy.wait()

    for copy in outgoing:
        copy.wait_send()
    for peer in range(owners - 1):
        source = lax.rem(col + 1 + peer, owners)
        for src, dst, ssem, rsem in ((h_ref, g_ref, h_send_sem, h_recv_sem), (t_ref, u_ref, t_send_sem, t_recv_sem)):
            incoming = pltpu.make_async_remote_copy(
                src_ref=src.at[source],
                dst_ref=dst.at[source],
                send_sem=ssem.at[source],
                recv_sem=rsem.at[source],
                device_id=(me, source),
                device_id_type=MESH,
            )
            incoming.wait_recv()
    own.wait()
    own_h.wait()
    own_t.wait()


def exchange(w_down, h_send, t_send, replicas, owners, pieces=4):
    local_experts, rows, width = w_down.shape
    return pl.pallas_call(
        lambda *refs: exchange_kernel(replicas, owners, pieces, *refs),
        out_shape=(
            jax.ShapeDtypeStruct((local_experts, replicas, rows, width), w_down.dtype),
            jax.ShapeDtypeStruct(h_send.shape, h_send.dtype),
            jax.ShapeDtypeStruct(t_send.shape, t_send.dtype),
        ),
        in_specs=[pl.BlockSpec(memory_space=pl.ANY)] * 3,
        out_specs=(pl.BlockSpec(memory_space=pl.ANY),) * 3,
        scratch_shapes=[
            pltpu.SemaphoreType.DMA((3,)),
            pltpu.SemaphoreType.DMA((2, replicas // 2, pieces)),
            pltpu.SemaphoreType.DMA((2, replicas // 2, pieces)),
            pltpu.SemaphoreType.DMA((owners,)),
            pltpu.SemaphoreType.DMA((owners,)),
            pltpu.SemaphoreType.DMA((owners,)),
            pltpu.SemaphoreType.DMA((owners,)),
        ],
        compiler_params=pltpu.CompilerParams(collective_id=0, has_side_effects=True),
        cost_estimate=pl.CostEstimate(
            flops=0,
            bytes_accessed=2 * replicas * w_down.size * 2 + 2 * h_send.size * 2,
            transcendentals=0,
        ),
    )(w_down, h_send, t_send)


def slot_counts(ids, experts):
    routes = ids.shape[-1]
    onehot = (ids[..., None] == jnp.arange(experts, dtype=jnp.int32)).astype(jnp.bfloat16)
    lower = (jnp.arange(routes)[:, None] > jnp.arange(routes)[None, :]).astype(jnp.bfloat16)
    before = jnp.einsum("rq,...qe->...re", lower, onehot, preferred_element_type=jnp.float32)
    return jnp.sum(before * onehot.astype(jnp.float32), axis=-1).astype(jnp.int32)


def local(cotangent, saved_gate_up, route_ids, route_weights, w_down):
    tokens, top = route_ids.shape
    width = cotangent.shape[1]
    hidden_units = saved_gate_up.shape[2] // 2
    owners = lax.axis_size("expert")
    replicas = lax.axis_size("dp")
    me = lax.axis_index("expert")
    local_experts = w_down.shape[0]
    experts = local_experts * owners
    capacity = min(tokens, 2 * tokens * top // experts)
    routes = tokens * top

    cot_group = lax.all_gather(cotangent, "expert", axis=0, tiled=True)

    gate = saved_gate_up[:, :, :hidden_units].astype(jnp.float32)
    up = saved_gate_up[:, :, hidden_units:].astype(jnp.float32)
    sig = jax.nn.sigmoid(gate)
    act = gate * sig
    hidden = (act * up).astype(jnp.bfloat16)
    weights = route_weights[:, :, None]
    scaled = (weights * hidden.astype(jnp.float32)).astype(jnp.bfloat16)

    flat_ids = route_ids.reshape(routes)
    slot = slot_counts(flat_ids, experts)
    position = flat_ids * capacity + slot
    slot_ids = jnp.arange(experts * capacity, dtype=jnp.int32)
    match = position[None, :] == slot_ids[:, None]
    route_of_slot = jnp.sum(jnp.where(match, jnp.arange(routes, dtype=jnp.int32)[None, :], 0), axis=1)
    filled = jnp.any(match, axis=1)
    h_rows = jnp.where(filled[:, None], scaled.reshape(routes, hidden_units)[route_of_slot], jnp.zeros((), jnp.bfloat16))
    h_send = h_rows.reshape(owners, local_experts, capacity, hidden_units)

    t_send = jnp.where(filled, route_of_slot // top, -1).reshape(owners, 1, local_experts * capacity)
    full_down, h_got, t_got = exchange(w_down, h_send, t_send, replicas, owners)
    h_got, t_got, cot_group = lax.optimization_barrier((h_got, t_got, cot_group))
    pick = (t_got.reshape(owners, local_experts * capacity, 1)
            == jnp.arange(tokens, dtype=jnp.int32)[None, None, :]).astype(jnp.bfloat16)
    dy = jnp.einsum(
        "sct,std->scd", pick, cot_group.reshape(owners, tokens, width),
        preferred_element_type=jnp.bfloat16,
    ).reshape(owners, local_experts, capacity, width)

    grads = jnp.einsum(
        "sjcd,jfd->sjcf", dy, full_down.reshape(local_experts, hidden_units, width),
        preferred_element_type=jnp.float32,
    ).astype(jnp.bfloat16)
    grads, dy, h_got = lax.optimization_barrier((grads, dy, h_got))
    back = lax.all_to_all(grads, "expert", split_axis=0, concat_axis=0, tiled=True)
    parts = []
    for j in range(local_experts):
        part = jnp.einsum(
            "scf,scd->fd", h_got[:, j], dy[:, j], preferred_element_type=jnp.float32
        ).astype(jnp.bfloat16)
        parts.append(part.reshape(replicas, hidden_units // replicas, width))
    summed = lax.psum_scatter(jnp.stack(parts, axis=1), "dp", scatter_dimension=0, tiled=True)
    grad_down = summed[0].astype(jnp.float32)
    returned_rows = back.reshape(experts * capacity, hidden_units)[position]
    qf = returned_rows.reshape(tokens, top, hidden_units).astype(jnp.float32)
    route_grad = jnp.sum(qf * hidden.astype(jnp.float32), -1)
    d_hidden = weights * qf
    d_gate = d_hidden * up * sig * (1.0 + gate * (1.0 - sig))
    d_up = d_hidden * act
    grad_gate_up = jnp.concatenate([d_gate, d_up], -1).astype(jnp.bfloat16)
    return (grad_gate_up, route_grad, grad_down)


def solution(mesh):
    return jax.shard_map(
        local,
        mesh=mesh,
        in_specs=(
            P(("dp", "expert"), None),
            P(("dp", "expert"), None, None),
            P(("dp", "expert"), None),
            P(("dp", "expert"), None),
            P("expert", "dp", None),
        ),
        out_specs=(
            P(("dp", "expert"), None, None),
            P(("dp", "expert"), None),
            P("expert", "dp", None),
        ),
        check_vma=False,
    )
```

```python
import jax
import jax.numpy as jnp
from jax import lax
from jax.experimental import pallas as pl
from jax.experimental.pallas import tpu as pltpu
from jax.sharding import PartitionSpec as P

MESH = pl.DeviceIdType.MESH


def ring_dp(pos, replicas):
    pos = lax.rem(pos + 2 * replicas, replicas)
    z = pos // 2
    core = lax.rem(pos, 2)
    core = jnp.where(lax.rem(z, 2) == 0, core, 1 - core)
    return z * 2 + core


def ring_pos(dp):
    z = dp // 2
    core = lax.rem(dp, 2)
    return z * 2 + jnp.where(lax.rem(z, 2) == 0, core, 1 - core)


def exchange_kernel(replicas, owners, pieces, w_ref, h_ref, t_ref, o_ref, g_ref, u_ref, sems, send_sem,
                    recv_sem, h_send_sem, h_recv_sem, t_send_sem, t_recv_sem):
    me = lax.axis_index("dp")
    col = lax.axis_index("expert")
    pos = ring_pos(me)
    right = ring_dp(pos + 1, replicas)
    left = ring_dp(pos - 1, replicas)
    cols = w_ref.shape[2] // pieces

    barrier = pltpu.get_barrier_semaphore()
    for neighbour in (left, right):
        pl.semaphore_signal(barrier, inc=1, device_id=(neighbour, col), device_id_type=MESH)
    for peer in range(owners - 1):
        other = lax.rem(col + 1 + peer, owners)
        pl.semaphore_signal(barrier, inc=1, device_id=(me, other), device_id_type=MESH)
    pl.semaphore_wait(barrier, 2 + owners - 1)

    own = pltpu.make_async_copy(w_ref, o_ref.at[:, me], sems.at[0])
    own.start()
    own_h = pltpu.make_async_copy(h_ref.at[col], g_ref.at[col], sems.at[1])
    own_h.start()
    own_t = pltpu.make_async_copy(t_ref.at[col], u_ref.at[col], sems.at[2])
    own_t.start()
    outgoing = []
    for peer in range(owners - 1):
        other = lax.rem(col + 1 + peer, owners)
        for src, dst, ssem, rsem in ((h_ref, g_ref, h_send_sem, h_recv_sem), (t_ref, u_ref, t_send_sem, t_recv_sem)):
            copy = pltpu.make_async_remote_copy(
                src_ref=src.at[other],
                dst_ref=dst.at[col],
                send_sem=ssem.at[other],
                recv_sem=rsem.at[col],
                device_id=(me, other),
                device_id_type=MESH,
            )
            copy.start()
            outgoing.append(copy)

    hops = (replicas // 2, replicas - 1 - replicas // 2)
    for step in range(hops[0]):
        copies = []
        for way, (target, sign) in enumerate(((right, -1), (left, 1))):
            if step >= hops[way]:
                continue
            block = ring_dp(pos + sign * step, replicas)
            for piece in range(pieces):
                part = pl.ds(piece * cols, cols)
                src = w_ref.at[:, :, part] if step == 0 else o_ref.at[:, block, :, part]
                copy = pltpu.make_async_remote_copy(
                    src_ref=src,
                    dst_ref=o_ref.at[:, block, :, part],
                    send_sem=send_sem.at[way, step, piece],
                    recv_sem=recv_sem.at[way, step, piece],
                    device_id=(target, col),
                    device_id_type=MESH,
                )
                copy.start()
                copies.append(copy)
        for copy in copies:
            copy.wait()

    for copy in outgoing:
        copy.wait_send()
    for peer in range(owners - 1):
        source = lax.rem(col + 1 + peer, owners)
        for src, dst, ssem, rsem in ((h_ref, g_ref, h_send_sem, h_recv_sem), (t_ref, u_ref, t_send_sem, t_recv_sem)):
            incoming = pltpu.make_async_remote_copy(
                src_ref=src.at[source],
                dst_ref=dst.at[source],
                send_sem=ssem.at[source],
                recv_sem=rsem.at[source],
                device_id=(me, source),
                device_id_type=MESH,
            )
            incoming.wait_recv()
    own.wait()
    own_h.wait()
    own_t.wait()


def exchange(w_down, h_send, t_send, replicas, owners, pieces=4):
    local_experts, rows, width = w_down.shape
    return pl.pallas_call(
        lambda *refs: exchange_kernel(replicas, owners, pieces, *refs),
        out_shape=(
            jax.ShapeDtypeStruct((local_experts, replicas, rows, width), w_down.dtype),
            jax.ShapeDtypeStruct(h_send.shape, h_send.dtype),
            jax.ShapeDtypeStruct(t_send.shape, t_send.dtype),
        ),
        in_specs=[pl.BlockSpec(memory_space=pl.ANY)] * 3,
        out_specs=(pl.BlockSpec(memory_space=pl.ANY),) * 3,
        scratch_shapes=[
            pltpu.SemaphoreType.DMA((3,)),
            pltpu.SemaphoreType.DMA((2, replicas // 2, pieces)),
            pltpu.SemaphoreType.DMA((2, replicas // 2, pieces)),
            pltpu.SemaphoreType.DMA((owners,)),
            pltpu.SemaphoreType.DMA((owners,)),
            pltpu.SemaphoreType.DMA((owners,)),
            pltpu.SemaphoreType.DMA((owners,)),
        ],
        compiler_params=pltpu.CompilerParams(collective_id=0, has_side_effects=True),
        cost_estimate=pl.CostEstimate(
            flops=0,
            bytes_accessed=2 * replicas * w_down.size * 2 + 2 * h_send.size * 2,
            transcendentals=0,
        ),
    )(w_down, h_send, t_send)


def return_kernel(owners, dy_ref, w_ref, back_ref, gbuf, own_sem, send_sem, recv_sem):
    me = lax.axis_index("dp")
    col = lax.axis_index("expert")

    barrier = pltpu.get_barrier_semaphore()
    for peer in range(owners - 1):
        other = lax.rem(col + 1 + peer, owners)
        pl.semaphore_signal(barrier, inc=1, device_id=(me, other), device_id_type=MESH)
    pl.semaphore_wait(barrier, owners - 1)

    def send(source):
        return pltpu.make_async_remote_copy(
            src_ref=gbuf.at[source],
            dst_ref=back_ref.at[col],
            send_sem=send_sem.at[source],
            recv_sem=recv_sem.at[col],
            device_id=(me, source),
            device_id_type=MESH,
        )

    previous = None
    for step in range(owners):
        source = lax.rem(col + 1 + step, owners)
        for j in range(w_ref.shape[0]):
            gbuf[source, j] = lax.dot_general(
                dy_ref[source, j], w_ref[j], (((1,), (1,)), ((), ())),
                preferred_element_type=jnp.float32,
            ).astype(gbuf.dtype)
        if previous is not None:
            send(previous).start()
        previous = source
    own = pltpu.make_async_copy(gbuf.at[col], back_ref.at[col], own_sem)
    own.start()

    for peer in range(owners - 1):
        send(lax.rem(col + 1 + peer, owners)).wait_send()
    for peer in range(owners - 1):
        source = lax.rem(col + 1 + peer, owners)
        pltpu.make_async_remote_copy(
            src_ref=gbuf.at[source],
            dst_ref=back_ref.at[source],
            send_sem=send_sem.at[source],
            recv_sem=recv_sem.at[source],
            device_id=(me, source),
            device_id_type=MESH,
        ).wait_recv()
    own.wait()


def give_back(dy, full_down, owners):
    sources, local_experts, capacity, width = dy.shape
    hidden_units = full_down.shape[1]
    shape = (sources, local_experts, capacity, hidden_units)
    return pl.pallas_call(
        lambda *refs: return_kernel(owners, *refs),
        out_shape=jax.ShapeDtypeStruct(shape, dy.dtype),
        in_specs=[pl.BlockSpec(memory_space=pltpu.VMEM)] * 2,
        out_specs=pl.BlockSpec(memory_space=pl.ANY),
        scratch_shapes=[
            pltpu.VMEM(shape, dy.dtype),
            pltpu.SemaphoreType.DMA(()),
            pltpu.SemaphoreType.DMA((owners,)),
            pltpu.SemaphoreType.DMA((owners,)),
        ],
        compiler_params=pltpu.CompilerParams(
            collective_id=1, has_side_effects=True, vmem_limit_bytes=48 * 1024 * 1024
        ),
        cost_estimate=pl.CostEstimate(
            flops=2 * sources * local_experts * capacity * width * hidden_units,
            bytes_accessed=(dy.size + full_down.size + 2 * sources * local_experts * capacity * hidden_units) * 2,
            transcendentals=0,
        ),
    )(dy, full_down)


def slot_counts(ids, experts):
    routes = ids.shape[-1]
    onehot = (ids[..., None] == jnp.arange(experts, dtype=jnp.int32)).astype(jnp.bfloat16)
    lower = (jnp.arange(routes)[:, None] > jnp.arange(routes)[None, :]).astype(jnp.bfloat16)
    before = jnp.einsum("rq,...qe->...re", lower, onehot, preferred_element_type=jnp.float32)
    return jnp.sum(before * onehot.astype(jnp.float32), axis=-1).astype(jnp.int32)


def local(cotangent, saved_gate_up, route_ids, route_weights, w_down):
    tokens, top = route_ids.shape
    width = cotangent.shape[1]
    hidden_units = saved_gate_up.shape[2] // 2
    owners = lax.axis_size("expert")
    replicas = lax.axis_size("dp")
    me = lax.axis_index("expert")
    local_experts = w_down.shape[0]
    experts = local_experts * owners
    capacity = min(tokens, 2 * tokens * top // experts)
    routes = tokens * top

    cot_group = lax.all_gather(cotangent, "expert", axis=0, tiled=True)

    gate = saved_gate_up[:, :, :hidden_units].astype(jnp.float32)
    up = saved_gate_up[:, :, hidden_units:].astype(jnp.float32)
    sig = jax.nn.sigmoid(gate)
    act = gate * sig
    hidden = (act * up).astype(jnp.bfloat16)
    weights = route_weights[:, :, None]
    scaled = (weights * hidden.astype(jnp.float32)).astype(jnp.bfloat16)

    flat_ids = route_ids.reshape(routes)
    slot = slot_counts(flat_ids, experts)
    position = flat_ids * capacity + slot
    slot_ids = jnp.arange(experts * capacity, dtype=jnp.int32)
    match = position[None, :] == slot_ids[:, None]
    route_of_slot = jnp.sum(jnp.where(match, jnp.arange(routes, dtype=jnp.int32)[None, :], 0), axis=1)
    filled = jnp.any(match, axis=1)
    h_rows = jnp.where(filled[:, None], scaled.reshape(routes, hidden_units)[route_of_slot], jnp.zeros((), jnp.bfloat16))
    h_send = h_rows.reshape(owners, local_experts, capacity, hidden_units)

    t_send = jnp.where(filled, route_of_slot // top, -1).reshape(owners, 1, local_experts * capacity)
    full_down, h_got, t_got = exchange(w_down, h_send, t_send, replicas, owners)
    h_got, t_got, cot_group = lax.optimization_barrier((h_got, t_got, cot_group))
    pick = (t_got.reshape(owners, local_experts * capacity, 1)
            == jnp.arange(tokens, dtype=jnp.int32)[None, None, :]).astype(jnp.bfloat16)
    dy = jnp.einsum(
        "sct,std->scd", pick, cot_group.reshape(owners, tokens, width),
        preferred_element_type=jnp.bfloat16,
    ).reshape(owners, local_experts, capacity, width)

    parts = []
    for j in range(local_experts):
        part = jnp.einsum(
            "scf,scd->fd", h_got[:, j], dy[:, j], preferred_element_type=jnp.float32
        ).astype(jnp.bfloat16)
        parts.append(part.reshape(replicas, hidden_units // replicas, width))
    stacked = jnp.stack(parts, axis=1)
    stacked, dy = lax.optimization_barrier((stacked, dy))
    summed = lax.psum_scatter(stacked, "dp", scatter_dimension=0, tiled=True)
    grad_down = summed[0].astype(jnp.float32)
    back = give_back(dy, full_down.reshape(local_experts, hidden_units, width), owners)
    returned_rows = back.reshape(experts * capacity, hidden_units)[position]
    qf = returned_rows.reshape(tokens, top, hidden_units).astype(jnp.float32)
    route_grad = jnp.sum(qf * hidden.astype(jnp.float32), -1)
    d_hidden = weights * qf
    d_gate = d_hidden * up * sig * (1.0 + gate * (1.0 - sig))
    d_up = d_hidden * act
    grad_gate_up = jnp.concatenate([d_gate, d_up], -1).astype(jnp.bfloat16)
    return (grad_gate_up, route_grad, grad_down)


def solution(mesh):
    return jax.shard_map(
        local,
        mesh=mesh,
        in_specs=(
            P(("dp", "expert"), None),
            P(("dp", "expert"), None, None),
            P(("dp", "expert"), None),
            P(("dp", "expert"), None),
            P("expert", "dp", None),
        ),
        out_specs=(
            P(("dp", "expert"), None, None),
            P(("dp", "expert"), None),
            P("expert", "dp", None),
        ),
        check_vma=False,
    )
```

```python
import jax
import jax.numpy as jnp
from jax import lax
from jax.experimental import pallas as pl
from jax.experimental.pallas import tpu as pltpu
from jax.sharding import PartitionSpec as P

MESH = pl.DeviceIdType.MESH


def ring_dp(pos, replicas):
    pos = lax.rem(pos + 2 * replicas, replicas)
    z = pos // 2
    core = lax.rem(pos, 2)
    core = jnp.where(lax.rem(z, 2) == 0, core, 1 - core)
    return z * 2 + core


def ring_pos(dp):
    z = dp // 2
    core = lax.rem(dp, 2)
    return z * 2 + jnp.where(lax.rem(z, 2) == 0, core, 1 - core)


def exchange_kernel(replicas, owners, pieces, w_ref, h_ref, t_ref, o_ref, g_ref, u_ref, sems, send_sem,
                    recv_sem, h_send_sem, h_recv_sem, t_send_sem, t_recv_sem):
    me = lax.axis_index("dp")
    col = lax.axis_index("expert")
    pos = ring_pos(me)
    right = ring_dp(pos + 1, replicas)
    left = ring_dp(pos - 1, replicas)
    cols = w_ref.shape[2] // pieces

    barrier = pltpu.get_barrier_semaphore()
    for neighbour in (left, right):
        pl.semaphore_signal(barrier, inc=1, device_id=(neighbour, col), device_id_type=MESH)
    for peer in range(owners - 1):
        other = lax.rem(col + 1 + peer, owners)
        pl.semaphore_signal(barrier, inc=1, device_id=(me, other), device_id_type=MESH)
    pl.semaphore_wait(barrier, 2 + owners - 1)

    own = pltpu.make_async_copy(w_ref, o_ref.at[:, me], sems.at[0])
    own.start()
    own_h = pltpu.make_async_copy(h_ref.at[col], g_ref.at[col], sems.at[1])
    own_h.start()
    own_t = pltpu.make_async_copy(t_ref.at[col], u_ref.at[col], sems.at[2])
    own_t.start()
    outgoing = []
    for peer in range(owners - 1):
        other = lax.rem(col + 1 + peer, owners)
        for src, dst, ssem, rsem in ((h_ref, g_ref, h_send_sem, h_recv_sem), (t_ref, u_ref, t_send_sem, t_recv_sem)):
            copy = pltpu.make_async_remote_copy(
                src_ref=src.at[other],
                dst_ref=dst.at[col],
                send_sem=ssem.at[other],
                recv_sem=rsem.at[col],
                device_id=(me, other),
                device_id_type=MESH,
            )
            copy.start()
            outgoing.append(copy)

    hops = (replicas // 2, replicas - 1 - replicas // 2)
    for step in range(hops[0]):
        copies = []
        for way, (target, sign) in enumerate(((right, -1), (left, 1))):
            if step >= hops[way]:
                continue
            block = ring_dp(pos + sign * step, replicas)
            for piece in range(pieces):
                part = pl.ds(piece * cols, cols)
                src = w_ref.at[:, :, part] if step == 0 else o_ref.at[:, block, :, part]
                copy = pltpu.make_async_remote_copy(
                    src_ref=src,
                    dst_ref=o_ref.at[:, block, :, part],
                    send_sem=send_sem.at[way, step, piece],
                    recv_sem=recv_sem.at[way, step, piece],
                    device_id=(target, col),
                    device_id_type=MESH,
                )
                copy.start()
                copies.append(copy)
        for copy in copies:
            copy.wait()

    for copy in outgoing:
        copy.wait_send()
    for peer in range(owners - 1):
        source = lax.rem(col + 1 + peer, owners)
        for src, dst, ssem, rsem in ((h_ref, g_ref, h_send_sem, h_recv_sem), (t_ref, u_ref, t_send_sem, t_recv_sem)):
            incoming = pltpu.make_async_remote_copy(
                src_ref=src.at[source],
                dst_ref=dst.at[source],
                send_sem=ssem.at[source],
                recv_sem=rsem.at[source],
                device_id=(me, source),
                device_id_type=MESH,
            )
            incoming.wait_recv()
    own.wait()
    own_h.wait()
    own_t.wait()


def exchange(w_down, h_send, t_send, replicas, owners, pieces=4):
    local_experts, rows, width = w_down.shape
    return pl.pallas_call(
        lambda *refs: exchange_kernel(replicas, owners, pieces, *refs),
        out_shape=(
            jax.ShapeDtypeStruct((local_experts, replicas, rows, width), w_down.dtype),
            jax.ShapeDtypeStruct(h_send.shape, h_send.dtype),
            jax.ShapeDtypeStruct(t_send.shape, t_send.dtype),
        ),
        in_specs=[pl.BlockSpec(memory_space=pl.ANY)] * 3,
        out_specs=(pl.BlockSpec(memory_space=pl.ANY),) * 3,
        scratch_shapes=[
            pltpu.SemaphoreType.DMA((3,)),
            pltpu.SemaphoreType.DMA((2, replicas // 2, pieces)),
            pltpu.SemaphoreType.DMA((2, replicas // 2, pieces)),
            pltpu.SemaphoreType.DMA((owners,)),
            pltpu.SemaphoreType.DMA((owners,)),
            pltpu.SemaphoreType.DMA((owners,)),
            pltpu.SemaphoreType.DMA((owners,)),
        ],
        compiler_params=pltpu.CompilerParams(collective_id=0, has_side_effects=True),
        cost_estimate=pl.CostEstimate(
            flops=0,
            bytes_accessed=2 * replicas * w_down.size * 2 + 2 * h_send.size * 2,
            transcendentals=0,
        ),
    )(w_down, h_send, t_send)


def return_kernel(owners, dy_ref, w_ref, back_ref, gbuf, own_sem, send_sem, recv_sem):
    me = lax.axis_index("dp")
    col = lax.axis_index("expert")
    local_experts = w_ref.shape[0]

    barrier = pltpu.get_barrier_semaphore()
    for peer in range(owners - 1):
        other = lax.rem(col + 1 + peer, owners)
        pl.semaphore_signal(barrier, inc=1, device_id=(me, other), device_id_type=MESH)
    pl.semaphore_wait(barrier, owners - 1)

    def send(source, j):
        return pltpu.make_async_remote_copy(
            src_ref=gbuf.at[source, j],
            dst_ref=back_ref.at[col, j],
            send_sem=send_sem.at[source, j],
            recv_sem=recv_sem.at[col, j],
            device_id=(me, source),
            device_id_type=MESH,
        )

    def step(i, carry):
        source = lax.rem(col + 1 + i, owners)
        for j in range(local_experts):
            gbuf[source, j] = lax.dot_general(
                dy_ref[source, j], w_ref[j], (((1,), (1,)), ((), ())),
                preferred_element_type=jnp.float32,
            ).astype(gbuf.dtype)

        @pl.when(i > 0)
        def _():
            previous = lax.rem(col + i, owners)
            for j in range(local_experts):
                send(previous, j).start()

        return carry

    lax.fori_loop(0, owners, step, 0)
    own = pltpu.make_async_copy(gbuf.at[col], back_ref.at[col], own_sem)
    own.start()

    def finish(peer, carry):
        other = lax.rem(col + 1 + peer, owners)
        for j in range(local_experts):
            send(other, j).wait_send()
        for j in range(local_experts):
            pltpu.make_async_remote_copy(
                src_ref=gbuf.at[other, j],
                dst_ref=back_ref.at[other, j],
                send_sem=send_sem.at[other, j],
                recv_sem=recv_sem.at[other, j],
                device_id=(me, other),
                device_id_type=MESH,
            ).wait_recv()
        return carry

    lax.fori_loop(0, owners - 1, finish, 0)
    own.wait()


def give_back(dy, full_down, owners):
    sources, local_experts, capacity, width = dy.shape
    hidden_units = full_down.shape[1]
    shape = (sources, local_experts, capacity, hidden_units)
    return pl.pallas_call(
        lambda *refs: return_kernel(owners, *refs),
        out_shape=jax.ShapeDtypeStruct(shape, dy.dtype),
        in_specs=[pl.BlockSpec(memory_space=pltpu.VMEM)] * 2,
        out_specs=pl.BlockSpec(memory_space=pl.ANY),
        scratch_shapes=[
            pltpu.VMEM(shape, dy.dtype),
            pltpu.SemaphoreType.DMA(()),
            pltpu.SemaphoreType.DMA((owners, local_experts)),
            pltpu.SemaphoreType.DMA((owners, local_experts)),
        ],
        compiler_params=pltpu.CompilerParams(
            collective_id=1, has_side_effects=True, vmem_limit_bytes=48 * 1024 * 1024
        ),
        cost_estimate=pl.CostEstimate(
            flops=2 * sources * local_experts * capacity * width * hidden_units,
            bytes_accessed=(dy.size + full_down.size + 2 * sources * local_experts * capacity * hidden_units) * 2,
            transcendentals=0,
        ),
    )(dy, full_down)


def slot_counts(ids, experts):
    routes = ids.shape[-1]
    onehot = (ids[..., None] == jnp.arange(experts, dtype=jnp.int32)).astype(jnp.bfloat16)
    lower = (jnp.arange(routes)[:, None] > jnp.arange(routes)[None, :]).astype(jnp.bfloat16)
    before = jnp.einsum("rq,...qe->...re", lower, onehot, preferred_element_type=jnp.float32)
    return jnp.sum(before * onehot.astype(jnp.float32), axis=-1).astype(jnp.int32)


def local(cotangent, saved_gate_up, route_ids, route_weights, w_down):
    tokens, top = route_ids.shape
    width = cotangent.shape[1]
    hidden_units = saved_gate_up.shape[2] // 2
    owners = lax.axis_size("expert")
    replicas = lax.axis_size("dp")
    me = lax.axis_index("expert")
    local_experts = w_down.shape[0]
    experts = local_experts * owners
    capacity = min(tokens, 2 * tokens * top // experts)
    routes = tokens * top

    cot_group = lax.all_gather(cotangent, "expert", axis=0, tiled=True)

    gate = saved_gate_up[:, :, :hidden_units].astype(jnp.float32)
    up = saved_gate_up[:, :, hidden_units:].astype(jnp.float32)
    sig = jax.nn.sigmoid(gate)
    act = gate * sig
    hidden = (act * up).astype(jnp.bfloat16)
    weights = route_weights[:, :, None]
    scaled = (weights * hidden.astype(jnp.float32)).astype(jnp.bfloat16)

    flat_ids = route_ids.reshape(routes)
    slot = slot_counts(flat_ids, experts)
    position = flat_ids * capacity + slot
    slot_ids = jnp.arange(experts * capacity, dtype=jnp.int32)
    match = position[None, :] == slot_ids[:, None]
    route_of_slot = jnp.sum(jnp.where(match, jnp.arange(routes, dtype=jnp.int32)[None, :], 0), axis=1)
    filled = jnp.any(match, axis=1)
    h_rows = jnp.where(filled[:, None], scaled.reshape(routes, hidden_units)[route_of_slot], jnp.zeros((), jnp.bfloat16))
    h_send = h_rows.reshape(owners, local_experts, capacity, hidden_units)

    t_send = jnp.where(filled, route_of_slot // top, -1).reshape(owners, 1, local_experts * capacity)
    full_down, h_got, t_got = exchange(w_down, h_send, t_send, replicas, owners)
    h_got, t_got, cot_group = lax.optimization_barrier((h_got, t_got, cot_group))
    pick = (t_got.reshape(owners, local_experts * capacity, 1)
            == jnp.arange(tokens, dtype=jnp.int32)[None, None, :]).astype(jnp.bfloat16)
    dy = jnp.einsum(
        "sct,std->scd", pick, cot_group.reshape(owners, tokens, width),
        preferred_element_type=jnp.bfloat16,
    ).reshape(owners, local_experts, capacity, width)

    parts = []
    for j in range(local_experts):
        part = jnp.einsum(
            "scf,scd->fd", h_got[:, j], dy[:, j], preferred_element_type=jnp.float32
        ).astype(jnp.bfloat16)
        parts.append(part.reshape(replicas, hidden_units // replicas, width))
    stacked = jnp.stack(parts, axis=1)
    stacked, dy = lax.optimization_barrier((stacked, dy))
    summed = lax.psum_scatter(stacked, "dp", scatter_dimension=0, tiled=True)
    grad_down = summed[0].astype(jnp.float32)
    back = give_back(dy, full_down.reshape(local_experts, hidden_units, width), owners)
    returned_rows = back.reshape(experts * capacity, hidden_units)[position]
    qf = returned_rows.reshape(tokens, top, hidden_units).astype(jnp.float32)
    route_grad = jnp.sum(qf * hidden.astype(jnp.float32), -1)
    d_hidden = weights * qf
    d_gate = d_hidden * up * sig * (1.0 + gate * (1.0 - sig))
    d_up = d_hidden * act
    grad_gate_up = jnp.concatenate([d_gate, d_up], -1).astype(jnp.bfloat16)
    return (grad_gate_up, route_grad, grad_down)


def solution(mesh):
    return jax.shard_map(
        local,
        mesh=mesh,
        in_specs=(
            P(("dp", "expert"), None),
            P(("dp", "expert"), None, None),
            P(("dp", "expert"), None),
            P(("dp", "expert"), None),
            P("expert", "dp", None),
        ),
        out_specs=(
            P(("dp", "expert"), None, None),
            P(("dp", "expert"), None),
            P("expert", "dp", None),
        ),
        check_vma=False,
    )
```

```python
import jax
import jax.numpy as jnp
from jax import lax
from jax.experimental import pallas as pl
from jax.experimental.pallas import tpu as pltpu
from jax.sharding import PartitionSpec as P

MESH = pl.DeviceIdType.MESH


def ring_dp(pos, replicas):
    pos = lax.rem(pos + 2 * replicas, replicas)
    z = pos // 2
    core = lax.rem(pos, 2)
    core = jnp.where(lax.rem(z, 2) == 0, core, 1 - core)
    return z * 2 + core


def ring_pos(dp):
    z = dp // 2
    core = lax.rem(dp, 2)
    return z * 2 + jnp.where(lax.rem(z, 2) == 0, core, 1 - core)


def exchange_kernel(replicas, owners, pieces, w_ref, h_ref, t_ref, o_ref, g_ref, u_ref, sems, send_sem,
                    recv_sem, h_send_sem, h_recv_sem, t_send_sem, t_recv_sem):
    me = lax.axis_index("dp")
    col = lax.axis_index("expert")
    pos = ring_pos(me)
    right = ring_dp(pos + 1, replicas)
    left = ring_dp(pos - 1, replicas)
    cols = w_ref.shape[2] // pieces

    barrier = pltpu.get_barrier_semaphore()
    for neighbour in (left, right):
        pl.semaphore_signal(barrier, inc=1, device_id=(neighbour, col), device_id_type=MESH)
    for peer in range(owners - 1):
        other = lax.rem(col + 1 + peer, owners)
        pl.semaphore_signal(barrier, inc=1, device_id=(me, other), device_id_type=MESH)
    pl.semaphore_wait(barrier, 2 + owners - 1)

    own = pltpu.make_async_copy(w_ref, o_ref.at[:, me], sems.at[0])
    own.start()
    own_h = pltpu.make_async_copy(h_ref.at[col], g_ref.at[col], sems.at[1])
    own_h.start()
    own_t = pltpu.make_async_copy(t_ref.at[col], u_ref.at[col], sems.at[2])
    own_t.start()
    outgoing = []
    for peer in range(owners - 1):
        other = lax.rem(col + 1 + peer, owners)
        for src, dst, ssem, rsem in ((h_ref, g_ref, h_send_sem, h_recv_sem), (t_ref, u_ref, t_send_sem, t_recv_sem)):
            copy = pltpu.make_async_remote_copy(
                src_ref=src.at[other],
                dst_ref=dst.at[col],
                send_sem=ssem.at[other],
                recv_sem=rsem.at[col],
                device_id=(me, other),
                device_id_type=MESH,
            )
            copy.start()
            outgoing.append(copy)

    hops = (replicas // 2, replicas - 1 - replicas // 2)
    for step in range(hops[0]):
        copies = []
        for way, (target, sign) in enumerate(((right, -1), (left, 1))):
            if step >= hops[way]:
                continue
            block = ring_dp(pos + sign * step, replicas)
            for piece in range(pieces):
                part = pl.ds(piece * cols, cols)
                src = w_ref.at[:, :, part] if step == 0 else o_ref.at[:, block, :, part]
                copy = pltpu.make_async_remote_copy(
                    src_ref=src,
                    dst_ref=o_ref.at[:, block, :, part],
                    send_sem=send_sem.at[way, step, piece],
                    recv_sem=recv_sem.at[way, step, piece],
                    device_id=(target, col),
                    device_id_type=MESH,
                )
                copy.start()
                copies.append(copy)
        for copy in copies:
            copy.wait()

    for copy in outgoing:
        copy.wait_send()
    for peer in range(owners - 1):
        source = lax.rem(col + 1 + peer, owners)
        for src, dst, ssem, rsem in ((h_ref, g_ref, h_send_sem, h_recv_sem), (t_ref, u_ref, t_send_sem, t_recv_sem)):
            incoming = pltpu.make_async_remote_copy(
                src_ref=src.at[source],
                dst_ref=dst.at[source],
                send_sem=ssem.at[source],
                recv_sem=rsem.at[source],
                device_id=(me, source),
                device_id_type=MESH,
            )
            incoming.wait_recv()
    own.wait()
    own_h.wait()
    own_t.wait()


def exchange(w_down, h_send, t_send, replicas, owners, pieces=4):
    local_experts, rows, width = w_down.shape
    return pl.pallas_call(
        lambda *refs: exchange_kernel(replicas, owners, pieces, *refs),
        out_shape=(
            jax.ShapeDtypeStruct((local_experts, replicas, rows, width), w_down.dtype),
            jax.ShapeDtypeStruct(h_send.shape, h_send.dtype),
            jax.ShapeDtypeStruct(t_send.shape, t_send.dtype),
        ),
        in_specs=[pl.BlockSpec(memory_space=pl.ANY)] * 3,
        out_specs=(pl.BlockSpec(memory_space=pl.ANY),) * 3,
        scratch_shapes=[
            pltpu.SemaphoreType.DMA((3,)),
            pltpu.SemaphoreType.DMA((2, replicas // 2, pieces)),
            pltpu.SemaphoreType.DMA((2, replicas // 2, pieces)),
            pltpu.SemaphoreType.DMA((owners,)),
            pltpu.SemaphoreType.DMA((owners,)),
            pltpu.SemaphoreType.DMA((owners,)),
            pltpu.SemaphoreType.DMA((owners,)),
        ],
        compiler_params=pltpu.CompilerParams(collective_id=0, has_side_effects=True),
        cost_estimate=pl.CostEstimate(
            flops=0,
            bytes_accessed=2 * replicas * w_down.size * 2 + 2 * h_send.size * 2,
            transcendentals=0,
        ),
    )(w_down, h_send, t_send)


def return_kernel(owners, pieces, dy_ref, w_ref, back_ref, gbuf, own_sem, send_sem, recv_sem):
    me = lax.axis_index("dp")
    col = lax.axis_index("expert")
    local_experts = w_ref.shape[0]

    barrier = pltpu.get_barrier_semaphore()
    for peer in range(owners - 1):
        other = lax.rem(col + 1 + peer, owners)
        pl.semaphore_signal(barrier, inc=1, device_id=(me, other), device_id_type=MESH)
    pl.semaphore_wait(barrier, owners - 1)

    rows = gbuf.shape[2] // pieces

    def send(source, j, piece):
        part = pl.ds(piece * rows, rows)
        return pltpu.make_async_remote_copy(
            src_ref=gbuf.at[source, j, part],
            dst_ref=back_ref.at[col, j, part],
            send_sem=send_sem.at[source, j, piece],
            recv_sem=recv_sem.at[col, j, piece],
            device_id=(me, source),
            device_id_type=MESH,
        )

    def step(i, carry):
        source = lax.rem(col + 1 + i, owners)
        for j in range(local_experts):
            gbuf[source, j] = lax.dot_general(
                dy_ref[source, j], w_ref[j], (((1,), (1,)), ((), ())),
                preferred_element_type=jnp.float32,
            ).astype(gbuf.dtype)

        @pl.when(i > 0)
        def _():
            previous = lax.rem(col + i, owners)
            for j in range(local_experts):
                for piece in range(pieces):
                    send(previous, j, piece).start()

        return carry

    lax.fori_loop(0, owners, step, 0)
    own = pltpu.make_async_copy(gbuf.at[col], back_ref.at[col], own_sem)
    own.start()

    def finish(peer, carry):
        other = lax.rem(col + 1 + peer, owners)
        for j in range(local_experts):
            for piece in range(pieces):
                send(other, j, piece).wait_send()
        for j in range(local_experts):
            for piece in range(pieces):
                part = pl.ds(piece * rows, rows)
                pltpu.make_async_remote_copy(
                    src_ref=gbuf.at[other, j, part],
                    dst_ref=back_ref.at[other, j, part],
                    send_sem=send_sem.at[other, j, piece],
                    recv_sem=recv_sem.at[other, j, piece],
                    device_id=(me, other),
                    device_id_type=MESH,
                ).wait_recv()
        return carry

    lax.fori_loop(0, owners - 1, finish, 0)
    own.wait()


def give_back(dy, full_down, owners, pieces=2):
    sources, local_experts, capacity, width = dy.shape
    hidden_units = full_down.shape[1]
    shape = (sources, local_experts, capacity, hidden_units)
    return pl.pallas_call(
        lambda *refs: return_kernel(owners, pieces, *refs),
        out_shape=jax.ShapeDtypeStruct(shape, dy.dtype),
        in_specs=[pl.BlockSpec(memory_space=pltpu.VMEM)] * 2,
        out_specs=pl.BlockSpec(memory_space=pl.ANY),
        scratch_shapes=[
            pltpu.VMEM(shape, dy.dtype),
            pltpu.SemaphoreType.DMA(()),
            pltpu.SemaphoreType.DMA((owners, local_experts, pieces)),
            pltpu.SemaphoreType.DMA((owners, local_experts, pieces)),
        ],
        compiler_params=pltpu.CompilerParams(
            collective_id=1, has_side_effects=True, vmem_limit_bytes=48 * 1024 * 1024
        ),
        cost_estimate=pl.CostEstimate(
            flops=2 * sources * local_experts * capacity * width * hidden_units,
            bytes_accessed=(dy.size + full_down.size + 2 * sources * local_experts * capacity * hidden_units) * 2,
            transcendentals=0,
        ),
    )(dy, full_down)


def slot_counts(ids, experts):
    routes = ids.shape[-1]
    onehot = (ids[..., None] == jnp.arange(experts, dtype=jnp.int32)).astype(jnp.bfloat16)
    lower = (jnp.arange(routes)[:, None] > jnp.arange(routes)[None, :]).astype(jnp.bfloat16)
    before = jnp.einsum("rq,...qe->...re", lower, onehot, preferred_element_type=jnp.float32)
    return jnp.sum(before * onehot.astype(jnp.float32), axis=-1).astype(jnp.int32)


def local(cotangent, saved_gate_up, route_ids, route_weights, w_down):
    tokens, top = route_ids.shape
    width = cotangent.shape[1]
    hidden_units = saved_gate_up.shape[2] // 2
    owners = lax.axis_size("expert")
    replicas = lax.axis_size("dp")
    me = lax.axis_index("expert")
    local_experts = w_down.shape[0]
    experts = local_experts * owners
    capacity = min(tokens, 2 * tokens * top // experts)
    routes = tokens * top

    cot_group = lax.all_gather(cotangent, "expert", axis=0, tiled=True)

    gate = saved_gate_up[:, :, :hidden_units].astype(jnp.float32)
    up = saved_gate_up[:, :, hidden_units:].astype(jnp.float32)
    sig = jax.nn.sigmoid(gate)
    act = gate * sig
    hidden = (act * up).astype(jnp.bfloat16)
    weights = route_weights[:, :, None]
    scaled = (weights * hidden.astype(jnp.float32)).astype(jnp.bfloat16)

    flat_ids = route_ids.reshape(routes)
    slot = slot_counts(flat_ids, experts)
    position = flat_ids * capacity + slot
    slot_ids = jnp.arange(experts * capacity, dtype=jnp.int32)
    match = position[None, :] == slot_ids[:, None]
    route_of_slot = jnp.sum(jnp.where(match, jnp.arange(routes, dtype=jnp.int32)[None, :], 0), axis=1)
    filled = jnp.any(match, axis=1)
    h_rows = jnp.where(filled[:, None], scaled.reshape(routes, hidden_units)[route_of_slot], jnp.zeros((), jnp.bfloat16))
    h_send = h_rows.reshape(owners, local_experts, capacity, hidden_units)

    t_send = jnp.where(filled, route_of_slot // top, -1).reshape(owners, 1, local_experts * capacity)
    full_down, h_got, t_got = exchange(w_down, h_send, t_send, replicas, owners)
    h_got, t_got, cot_group = lax.optimization_barrier((h_got, t_got, cot_group))
    pick = (t_got.reshape(owners, local_experts * capacity, 1)
            == jnp.arange(tokens, dtype=jnp.int32)[None, None, :]).astype(jnp.bfloat16)
    dy = jnp.einsum(
        "sct,std->scd", pick, cot_group.reshape(owners, tokens, width),
        preferred_element_type=jnp.bfloat16,
    ).reshape(owners, local_experts, capacity, width)

    parts = []
    for j in range(local_experts):
        part = jnp.einsum(
            "scf,scd->fd", h_got[:, j], dy[:, j], preferred_element_type=jnp.float32
        ).astype(jnp.bfloat16)
        parts.append(part.reshape(replicas, hidden_units // replicas, width))
    stacked = jnp.stack(parts, axis=1)
    stacked, dy = lax.optimization_barrier((stacked, dy))
    summed = lax.psum_scatter(stacked, "dp", scatter_dimension=0, tiled=True)
    grad_down = summed[0].astype(jnp.float32)
    back = give_back(dy, full_down.reshape(local_experts, hidden_units, width), owners)
    returned_rows = back.reshape(experts * capacity, hidden_units)[position]
    qf = returned_rows.reshape(tokens, top, hidden_units).astype(jnp.float32)
    route_grad = jnp.sum(qf * hidden.astype(jnp.float32), -1)
    d_hidden = weights * qf
    d_gate = d_hidden * up * sig * (1.0 + gate * (1.0 - sig))
    d_up = d_hidden * act
    grad_gate_up = jnp.concatenate([d_gate, d_up], -1).astype(jnp.bfloat16)
    return (grad_gate_up, route_grad, grad_down)


def solution(mesh):
    return jax.shard_map(
        local,
        mesh=mesh,
        in_specs=(
            P(("dp", "expert"), None),
            P(("dp", "expert"), None, None),
            P(("dp", "expert"), None),
            P(("dp", "expert"), None),
            P("expert", "dp", None),
        ),
        out_specs=(
            P(("dp", "expert"), None, None),
            P(("dp", "expert"), None),
            P("expert", "dp", None),
        ),
        check_vma=False,
    )
```

```python
import jax
import jax.numpy as jnp
from jax import lax
from jax.experimental import pallas as pl
from jax.experimental.pallas import tpu as pltpu
from jax.sharding import PartitionSpec as P

MESH = pl.DeviceIdType.MESH


def ring_dp(pos, replicas):
    pos = lax.rem(pos + 2 * replicas, replicas)
    z = pos // 2
    core = lax.rem(pos, 2)
    core = jnp.where(lax.rem(z, 2) == 0, core, 1 - core)
    return z * 2 + core


def ring_pos(dp):
    z = dp // 2
    core = lax.rem(dp, 2)
    return z * 2 + jnp.where(lax.rem(z, 2) == 0, core, 1 - core)


def exchange_kernel(replicas, owners, pieces, w_ref, h_ref, t_ref, o_ref, g_ref, u_ref, sems, send_sem,
                    recv_sem, h_send_sem, h_recv_sem, t_send_sem, t_recv_sem):
    me = lax.axis_index("dp")
    col = lax.axis_index("expert")
    pos = ring_pos(me)
    right = ring_dp(pos + 1, replicas)
    left = ring_dp(pos - 1, replicas)
    cols = w_ref.shape[2] // pieces

    barrier = pltpu.get_barrier_semaphore()
    for neighbour in (left, right):
        pl.semaphore_signal(barrier, inc=1, device_id=(neighbour, col), device_id_type=MESH)
    for peer in range(owners - 1):
        other = lax.rem(col + 1 + peer, owners)
        pl.semaphore_signal(barrier, inc=1, device_id=(me, other), device_id_type=MESH)
    pl.semaphore_wait(barrier, 2 + owners - 1)

    own = pltpu.make_async_copy(w_ref, o_ref.at[:, me], sems.at[0])
    own.start()
    own_h = pltpu.make_async_copy(h_ref.at[col], g_ref.at[col], sems.at[1])
    own_h.start()
    own_t = pltpu.make_async_copy(t_ref.at[col], u_ref.at[col], sems.at[2])
    own_t.start()
    outgoing = []
    for peer in range(owners - 1):
        other = lax.rem(col + 1 + peer, owners)
        for src, dst, ssem, rsem in ((h_ref, g_ref, h_send_sem, h_recv_sem), (t_ref, u_ref, t_send_sem, t_recv_sem)):
            copy = pltpu.make_async_remote_copy(
                src_ref=src.at[other],
                dst_ref=dst.at[col],
                send_sem=ssem.at[other],
                recv_sem=rsem.at[col],
                device_id=(me, other),
                device_id_type=MESH,
            )
            copy.start()
            outgoing.append(copy)

    hops = (replicas // 2, replicas - 1 - replicas // 2)
    for step in range(hops[0]):
        copies = []
        for way, (target, sign) in enumerate(((right, -1), (left, 1))):
            if step >= hops[way]:
                continue
            block = ring_dp(pos + sign * step, replicas)
            for piece in range(pieces):
                part = pl.ds(piece * cols, cols)
                src = w_ref.at[:, :, part] if step == 0 else o_ref.at[:, block, :, part]
                copy = pltpu.make_async_remote_copy(
                    src_ref=src,
                    dst_ref=o_ref.at[:, block, :, part],
                    send_sem=send_sem.at[way, step, piece],
                    recv_sem=recv_sem.at[way, step, piece],
                    device_id=(target, col),
                    device_id_type=MESH,
                )
                copy.start()
                copies.append(copy)
        for copy in copies:
            copy.wait()

    for copy in outgoing:
        copy.wait_send()
    for peer in range(owners - 1):
        source = lax.rem(col + 1 + peer, owners)
        for src, dst, ssem, rsem in ((h_ref, g_ref, h_send_sem, h_recv_sem), (t_ref, u_ref, t_send_sem, t_recv_sem)):
            incoming = pltpu.make_async_remote_copy(
                src_ref=src.at[source],
                dst_ref=dst.at[source],
                send_sem=ssem.at[source],
                recv_sem=rsem.at[source],
                device_id=(me, source),
                device_id_type=MESH,
            )
            incoming.wait_recv()
    own.wait()
    own_h.wait()
    own_t.wait()


def exchange(w_down, h_send, t_send, replicas, owners, pieces=4):
    local_experts, rows, width = w_down.shape
    return pl.pallas_call(
        lambda *refs: exchange_kernel(replicas, owners, pieces, *refs),
        out_shape=(
            jax.ShapeDtypeStruct((local_experts, replicas, rows, width), w_down.dtype),
            jax.ShapeDtypeStruct(h_send.shape, h_send.dtype),
            jax.ShapeDtypeStruct(t_send.shape, t_send.dtype),
        ),
        in_specs=[pl.BlockSpec(memory_space=pl.ANY)] * 3,
        out_specs=(pl.BlockSpec(memory_space=pl.ANY),) * 3,
        scratch_shapes=[
            pltpu.SemaphoreType.DMA((3,)),
            pltpu.SemaphoreType.DMA((2, replicas // 2, pieces)),
            pltpu.SemaphoreType.DMA((2, replicas // 2, pieces)),
            pltpu.SemaphoreType.DMA((owners,)),
            pltpu.SemaphoreType.DMA((owners,)),
            pltpu.SemaphoreType.DMA((owners,)),
            pltpu.SemaphoreType.DMA((owners,)),
        ],
        compiler_params=pltpu.CompilerParams(collective_id=0, has_side_effects=True),
        cost_estimate=pl.CostEstimate(
            flops=0,
            bytes_accessed=2 * replicas * w_down.size * 2 + 2 * h_send.size * 2,
            transcendentals=0,
        ),
    )(w_down, h_send, t_send)


def return_kernel(owners, dy_ref, w_ref, back_ref, gbuf, own_sem, send_sem, recv_sem):
    me = lax.axis_index("dp")
    col = lax.axis_index("expert")
    local_experts = w_ref.shape[0]

    barrier = pltpu.get_barrier_semaphore()
    for peer in range(owners - 1):
        other = lax.rem(col + 1 + peer, owners)
        pl.semaphore_signal(barrier, inc=1, device_id=(me, other), device_id_type=MESH)
    pl.semaphore_wait(barrier, owners - 1)

    def send(source, j):
        return pltpu.make_async_remote_copy(
            src_ref=gbuf.at[source, j],
            dst_ref=back_ref.at[col, j],
            send_sem=send_sem.at[source, j],
            recv_sem=recv_sem.at[col, j],
            device_id=(me, source),
            device_id_type=MESH,
        )

    def step(i, carry):
        source = lax.rem(col + 1 + i, owners)
        for j in range(local_experts):
            gbuf[source, j] = lax.dot_general(
                dy_ref[source, j], w_ref[j], (((1,), (1,)), ((), ())),
                preferred_element_type=jnp.float32,
            ).astype(gbuf.dtype)

        @pl.when(i > 0)
        def _():
            previous = lax.rem(col + i, owners)
            for j in range(local_experts):
                send(previous, j).start()

        return carry

    lax.fori_loop(0, owners, step, 0)
    own = pltpu.make_async_copy(gbuf.at[col], back_ref.at[col], own_sem)
    own.start()

    def finish(peer, carry):
        other = lax.rem(col + 1 + peer, owners)
        for j in range(local_experts):
            send(other, j).wait_send()
        for j in range(local_experts):
            pltpu.make_async_remote_copy(
                src_ref=gbuf.at[other, j],
                dst_ref=back_ref.at[other, j],
                send_sem=send_sem.at[other, j],
                recv_sem=recv_sem.at[other, j],
                device_id=(me, other),
                device_id_type=MESH,
            ).wait_recv()
        return carry

    lax.fori_loop(0, owners - 1, finish, 0)
    own.wait()


def give_back(dy, full_down, owners):
    sources, local_experts, capacity, width = dy.shape
    hidden_units = full_down.shape[1]
    shape = (sources, local_experts, capacity, hidden_units)
    return pl.pallas_call(
        lambda *refs: return_kernel(owners, *refs),
        out_shape=jax.ShapeDtypeStruct(shape, dy.dtype),
        in_specs=[pl.BlockSpec(memory_space=pltpu.VMEM)] * 2,
        out_specs=pl.BlockSpec(memory_space=pl.ANY),
        scratch_shapes=[
            pltpu.VMEM(shape, dy.dtype),
            pltpu.SemaphoreType.DMA(()),
            pltpu.SemaphoreType.DMA((owners, local_experts)),
            pltpu.SemaphoreType.DMA((owners, local_experts)),
        ],
        compiler_params=pltpu.CompilerParams(
            collective_id=1, has_side_effects=True, vmem_limit_bytes=48 * 1024 * 1024
        ),
        cost_estimate=pl.CostEstimate(
            flops=2 * sources * local_experts * capacity * width * hidden_units,
            bytes_accessed=(dy.size + full_down.size + 2 * sources * local_experts * capacity * hidden_units) * 2,
            transcendentals=0,
        ),
    )(dy, full_down)


def slot_counts(ids, experts):
    routes = ids.shape[-1]
    onehot = (ids[..., None] == jnp.arange(experts, dtype=jnp.int32)).astype(jnp.bfloat16)
    lower = (jnp.arange(routes)[:, None] > jnp.arange(routes)[None, :]).astype(jnp.bfloat16)
    before = jnp.einsum("rq,...qe->...re", lower, onehot, preferred_element_type=jnp.float32)
    return jnp.sum(before * onehot.astype(jnp.float32), axis=-1).astype(jnp.int32)


def local(cotangent, saved_gate_up, route_ids, route_weights, w_down):
    tokens, top = route_ids.shape
    width = cotangent.shape[1]
    hidden_units = saved_gate_up.shape[2] // 2
    owners = lax.axis_size("expert")
    replicas = lax.axis_size("dp")
    me = lax.axis_index("expert")
    local_experts = w_down.shape[0]
    experts = local_experts * owners
    capacity = min(tokens, 2 * tokens * top // experts)
    routes = tokens * top

    cot_group = lax.all_gather(cotangent, "expert", axis=0, tiled=True)

    gate = saved_gate_up[:, :, :hidden_units].astype(jnp.float32)
    up = saved_gate_up[:, :, hidden_units:].astype(jnp.float32)
    sig = jax.nn.sigmoid(gate)
    act = gate * sig
    hidden = (act * up).astype(jnp.bfloat16)
    weights = route_weights[:, :, None]
    scaled = (weights * hidden.astype(jnp.float32)).astype(jnp.bfloat16)

    flat_ids = route_ids.reshape(routes)
    slot = slot_counts(flat_ids, experts)
    position = flat_ids * capacity + slot
    slot_ids = jnp.arange(experts * capacity, dtype=jnp.int32)
    match = position[None, :] == slot_ids[:, None]
    route_of_slot = jnp.sum(jnp.where(match, jnp.arange(routes, dtype=jnp.int32)[None, :], 0), axis=1)
    filled = jnp.any(match, axis=1)
    h_rows = jnp.where(filled[:, None], scaled.reshape(routes, hidden_units)[route_of_slot], jnp.zeros((), jnp.bfloat16))
    h_send = h_rows.reshape(owners, local_experts, capacity, hidden_units)

    t_send = jnp.where(filled, route_of_slot // top, -1).reshape(owners, 1, local_experts * capacity)
    full_down, h_got, t_got = exchange(w_down, h_send, t_send, replicas, owners)
    h_got, t_got, cot_group = lax.optimization_barrier((h_got, t_got, cot_group))
    pick = (t_got.reshape(owners, local_experts * capacity, 1)
            == jnp.arange(tokens, dtype=jnp.int32)[None, None, :]).astype(jnp.bfloat16)
    dy = jnp.einsum(
        "sct,std->scd", pick, cot_group.reshape(owners, tokens, width),
        preferred_element_type=jnp.bfloat16,
    ).reshape(owners, local_experts, capacity, width)

    parts = []
    for j in range(local_experts):
        part = jnp.einsum(
            "scf,scd->fd", h_got[:, j], dy[:, j], preferred_element_type=jnp.float32
        ).astype(jnp.bfloat16)
        parts.append(part.reshape(replicas, hidden_units // replicas, width))
    stacked = jnp.stack(parts, axis=1)
    stacked, dy = lax.optimization_barrier((stacked, dy))
    summed = lax.psum_scatter(stacked, "dp", scatter_dimension=0, tiled=True)
    grad_down = summed[0].astype(jnp.float32)
    back = give_back(dy, full_down.reshape(local_experts, hidden_units, width), owners)
    returned_rows = back.reshape(experts * capacity, hidden_units)[position]
    qf = returned_rows.reshape(tokens, top, hidden_units).astype(jnp.float32)
    route_grad = jnp.sum(qf * hidden.astype(jnp.float32), -1)
    row = saved_gate_up.astype(jnp.float32)
    partner = jnp.roll(row, hidden_units, axis=-1)
    is_gate = jnp.arange(2 * hidden_units) < hidden_units
    g = jnp.where(is_gate, row, partner)
    u = jnp.where(is_gate, partner, row)
    s_g = jax.nn.sigmoid(g)
    d_both = weights * jnp.concatenate([qf, qf], -1)
    grad_gate_up = jnp.where(is_gate, d_both * u * s_g * (1.0 + g * (1.0 - s_g)), d_both * (g * s_g)).astype(jnp.bfloat16)
    return (grad_gate_up, route_grad, grad_down)


def solution(mesh):
    return jax.shard_map(
        local,
        mesh=mesh,
        in_specs=(
            P(("dp", "expert"), None),
            P(("dp", "expert"), None, None),
            P(("dp", "expert"), None),
            P(("dp", "expert"), None),
            P("expert", "dp", None),
        ),
        out_specs=(
            P(("dp", "expert"), None, None),
            P(("dp", "expert"), None),
            P("expert", "dp", None),
        ),
        check_vma=False,
    )
```

```python
import jax
import jax.numpy as jnp
from jax import lax
from jax.experimental import pallas as pl
from jax.experimental.pallas import tpu as pltpu
from jax.sharding import PartitionSpec as P

MESH = pl.DeviceIdType.MESH


def ring_dp(pos, replicas):
    pos = lax.rem(pos + 2 * replicas, replicas)
    z = pos // 2
    core = lax.rem(pos, 2)
    core = jnp.where(lax.rem(z, 2) == 0, core, 1 - core)
    return z * 2 + core


def ring_pos(dp):
    z = dp // 2
    core = lax.rem(dp, 2)
    return z * 2 + jnp.where(lax.rem(z, 2) == 0, core, 1 - core)


def exchange_kernel(replicas, owners, pieces, w_ref, h_ref, t_ref, o_ref, g_ref, u_ref, sems, send_sem,
                    recv_sem, h_send_sem, h_recv_sem, t_send_sem, t_recv_sem):
    me = lax.axis_index("dp")
    col = lax.axis_index("expert")
    pos = ring_pos(me)
    right = ring_dp(pos + 1, replicas)
    left = ring_dp(pos - 1, replicas)
    cols = w_ref.shape[2] // pieces

    barrier = pltpu.get_barrier_semaphore()
    for neighbour in (left, right):
        pl.semaphore_signal(barrier, inc=1, device_id=(neighbour, col), device_id_type=MESH)
    for peer in range(owners - 1):
        other = lax.rem(col + 1 + peer, owners)
        pl.semaphore_signal(barrier, inc=1, device_id=(me, other), device_id_type=MESH)
    pl.semaphore_wait(barrier, 2 + owners - 1)

    own = pltpu.make_async_copy(w_ref, o_ref.at[:, me], sems.at[0])
    own.start()
    own_h = pltpu.make_async_copy(h_ref.at[col], g_ref.at[col], sems.at[1])
    own_h.start()
    own_t = pltpu.make_async_copy(t_ref.at[col], u_ref.at[col], sems.at[2])
    own_t.start()
    outgoing = []
    for peer in range(owners - 1):
        other = lax.rem(col + 1 + peer, owners)
        for src, dst, ssem, rsem in ((h_ref, g_ref, h_send_sem, h_recv_sem), (t_ref, u_ref, t_send_sem, t_recv_sem)):
            copy = pltpu.make_async_remote_copy(
                src_ref=src.at[other],
                dst_ref=dst.at[col],
                send_sem=ssem.at[other],
                recv_sem=rsem.at[col],
                device_id=(me, other),
                device_id_type=MESH,
            )
            copy.start()
            outgoing.append(copy)

    hops = (replicas // 2, replicas - 1 - replicas // 2)
    for step in range(hops[0]):
        copies = []
        for way, (target, sign) in enumerate(((right, -1), (left, 1))):
            if step >= hops[way]:
                continue
            block = ring_dp(pos + sign * step, replicas)
            for piece in range(pieces):
                part = pl.ds(piece * cols, cols)
                src = w_ref.at[:, :, part] if step == 0 else o_ref.at[:, block, :, part]
                copy = pltpu.make_async_remote_copy(
                    src_ref=src,
                    dst_ref=o_ref.at[:, block, :, part],
                    send_sem=send_sem.at[way, step, piece],
                    recv_sem=recv_sem.at[way, step, piece],
                    device_id=(target, col),
                    device_id_type=MESH,
                )
                copy.start()
                copies.append(copy)
        for copy in copies:
            copy.wait()

    for copy in outgoing:
        copy.wait_send()
    for peer in range(owners - 1):
        source = lax.rem(col + 1 + peer, owners)
        for src, dst, ssem, rsem in ((h_ref, g_ref, h_send_sem, h_recv_sem), (t_ref, u_ref, t_send_sem, t_recv_sem)):
            incoming = pltpu.make_async_remote_copy(
                src_ref=src.at[source],
                dst_ref=dst.at[source],
                send_sem=ssem.at[source],
                recv_sem=rsem.at[source],
                device_id=(me, source),
                device_id_type=MESH,
            )
            incoming.wait_recv()
    own.wait()
    own_h.wait()
    own_t.wait()


def exchange(w_down, h_send, t_send, replicas, owners, pieces=4):
    local_experts, rows, width = w_down.shape
    return pl.pallas_call(
        lambda *refs: exchange_kernel(replicas, owners, pieces, *refs),
        out_shape=(
            jax.ShapeDtypeStruct((local_experts, replicas, rows, width), w_down.dtype),
            jax.ShapeDtypeStruct(h_send.shape, h_send.dtype),
            jax.ShapeDtypeStruct(t_send.shape, t_send.dtype),
        ),
        in_specs=[pl.BlockSpec(memory_space=pl.ANY)] * 3,
        out_specs=(pl.BlockSpec(memory_space=pl.ANY),) * 3,
        scratch_shapes=[
            pltpu.SemaphoreType.DMA((3,)),
            pltpu.SemaphoreType.DMA((2, replicas // 2, pieces)),
            pltpu.SemaphoreType.DMA((2, replicas // 2, pieces)),
            pltpu.SemaphoreType.DMA((owners,)),
            pltpu.SemaphoreType.DMA((owners,)),
            pltpu.SemaphoreType.DMA((owners,)),
            pltpu.SemaphoreType.DMA((owners,)),
        ],
        compiler_params=pltpu.CompilerParams(collective_id=0, has_side_effects=True),
        cost_estimate=pl.CostEstimate(
            flops=0,
            bytes_accessed=2 * replicas * w_down.size * 2 + 2 * h_send.size * 2,
            transcendentals=0,
        ),
    )(w_down, h_send, t_send)


def return_kernel(owners, dy_ref, w_ref, back_ref, gbuf, own_sem, send_sem, recv_sem):
    me = lax.axis_index("dp")
    col = lax.axis_index("expert")
    local_experts = w_ref.shape[0]

    barrier = pltpu.get_barrier_semaphore()
    for peer in range(owners - 1):
        other = lax.rem(col + 1 + peer, owners)
        pl.semaphore_signal(barrier, inc=1, device_id=(me, other), device_id_type=MESH)
    pl.semaphore_wait(barrier, owners - 1)

    def send(source, j):
        return pltpu.make_async_remote_copy(
            src_ref=gbuf.at[source, j],
            dst_ref=back_ref.at[col, j],
            send_sem=send_sem.at[source, j],
            recv_sem=recv_sem.at[col, j],
            device_id=(me, source),
            device_id_type=MESH,
        )

    def step(i, carry):
        source = lax.rem(col + 1 + i, owners)
        for j in range(local_experts):
            gbuf[source, j] = lax.dot_general(
                dy_ref[source, j], w_ref[j], (((1,), (1,)), ((), ())),
                preferred_element_type=jnp.float32,
            ).astype(gbuf.dtype)

        @pl.when(i > 0)
        def _():
            previous = lax.rem(col + i, owners)
            for j in range(local_experts):
                send(previous, j).start()

        return carry

    lax.fori_loop(0, owners, step, 0)
    own = pltpu.make_async_copy(gbuf.at[col], back_ref.at[col], own_sem)
    own.start()

    def finish(peer, carry):
        other = lax.rem(col + 1 + peer, owners)
        for j in range(local_experts):
            send(other, j).wait_send()
        for j in range(local_experts):
            pltpu.make_async_remote_copy(
                src_ref=gbuf.at[other, j],
                dst_ref=back_ref.at[other, j],
                send_sem=send_sem.at[other, j],
                recv_sem=recv_sem.at[other, j],
                device_id=(me, other),
                device_id_type=MESH,
            ).wait_recv()
        return carry

    lax.fori_loop(0, owners - 1, finish, 0)
    own.wait()


def give_back(dy, full_down, owners):
    sources, local_experts, capacity, width = dy.shape
    hidden_units = full_down.shape[1]
    shape = (sources, local_experts, capacity, hidden_units)
    return pl.pallas_call(
        lambda *refs: return_kernel(owners, *refs),
        out_shape=jax.ShapeDtypeStruct(shape, dy.dtype),
        in_specs=[pl.BlockSpec(memory_space=pltpu.VMEM)] * 2,
        out_specs=pl.BlockSpec(memory_space=pl.ANY),
        scratch_shapes=[
            pltpu.VMEM(shape, dy.dtype),
            pltpu.SemaphoreType.DMA(()),
            pltpu.SemaphoreType.DMA((owners, local_experts)),
            pltpu.SemaphoreType.DMA((owners, local_experts)),
        ],
        compiler_params=pltpu.CompilerParams(
            collective_id=1, has_side_effects=True, vmem_limit_bytes=48 * 1024 * 1024
        ),
        cost_estimate=pl.CostEstimate(
            flops=2 * sources * local_experts * capacity * width * hidden_units,
            bytes_accessed=(dy.size + full_down.size + 2 * sources * local_experts * capacity * hidden_units) * 2,
            transcendentals=0,
        ),
    )(dy, full_down)


def slot_counts(ids, experts):
    routes = ids.shape[-1]
    onehot = (ids[..., None] == jnp.arange(experts, dtype=jnp.int32)).astype(jnp.bfloat16)
    lower = (jnp.arange(routes)[:, None] > jnp.arange(routes)[None, :]).astype(jnp.bfloat16)
    before = jnp.einsum("rq,...qe->...re", lower, onehot, preferred_element_type=jnp.float32)
    return jnp.sum(before * onehot.astype(jnp.float32), axis=-1).astype(jnp.int32)


def local(cotangent, saved_gate_up, route_ids, route_weights, w_down):
    tokens, top = route_ids.shape
    width = cotangent.shape[1]
    hidden_units = saved_gate_up.shape[2] // 2
    owners = lax.axis_size("expert")
    replicas = lax.axis_size("dp")
    me = lax.axis_index("expert")
    local_experts = w_down.shape[0]
    experts = local_experts * owners
    capacity = min(tokens, 2 * tokens * top // experts)
    routes = tokens * top

    cot_group = lax.all_gather(cotangent, "expert", axis=0, tiled=True)

    gate = saved_gate_up[:, :, :hidden_units].astype(jnp.float32)
    up = saved_gate_up[:, :, hidden_units:].astype(jnp.float32)
    sig = jax.nn.sigmoid(gate)
    act = gate * sig
    hidden = (act * up).astype(jnp.bfloat16)
    weights = route_weights[:, :, None]
    scaled = (weights * hidden.astype(jnp.float32)).astype(jnp.bfloat16)

    flat_ids = route_ids.reshape(routes)
    slot = slot_counts(flat_ids, experts)
    position = flat_ids * capacity + slot
    slot_ids = jnp.arange(experts * capacity, dtype=jnp.int32)
    match = position[None, :] == slot_ids[:, None]
    route_of_slot = jnp.sum(jnp.where(match, jnp.arange(routes, dtype=jnp.int32)[None, :], 0), axis=1)
    filled = jnp.any(match, axis=1)
    h_rows = jnp.where(filled[:, None], scaled.reshape(routes, hidden_units)[route_of_slot], jnp.zeros((), jnp.bfloat16))
    h_send = h_rows.reshape(owners, local_experts, capacity, hidden_units)

    t_send = jnp.where(filled, route_of_slot // top, -1).reshape(owners, 1, local_experts * capacity)
    full_down, h_got, t_got = exchange(w_down, h_send, t_send, replicas, owners)
    h_got, t_got, cot_group = lax.optimization_barrier((h_got, t_got, cot_group))
    pick = (t_got.reshape(owners, local_experts * capacity, 1)
            == jnp.arange(tokens, dtype=jnp.int32)[None, None, :]).astype(jnp.bfloat16)
    dy = jnp.einsum(
        "sct,std->scd", pick, cot_group.reshape(owners, tokens, width),
        preferred_element_type=jnp.bfloat16,
    ).reshape(owners, local_experts, capacity, width)

    parts = []
    for j in range(local_experts):
        part = jnp.einsum(
            "scf,scd->fd", h_got[:, j], dy[:, j], preferred_element_type=jnp.float32
        ).astype(jnp.bfloat16)
        parts.append(part.reshape(replicas, hidden_units // replicas, width))
    stacked = jnp.stack(parts, axis=1)
    stacked, dy = lax.optimization_barrier((stacked, dy))
    summed = lax.psum_scatter(stacked, "dp", scatter_dimension=0, tiled=True)
    grad_down = summed[0].astype(jnp.float32)
    back = give_back(dy, full_down.reshape(local_experts, hidden_units, width), owners)
    take = (position.reshape(tokens, top, 1)
            == jnp.arange(experts * capacity, dtype=jnp.int32)[None, None, :]).astype(jnp.bfloat16)
    qf = jnp.einsum(
        "tkr,rf->tkf", take, back.reshape(experts * capacity, hidden_units),
        preferred_element_type=jnp.float32,
    )
    route_grad = jnp.sum(qf * hidden.astype(jnp.float32), -1)
    d_hidden = weights * qf
    d_gate = d_hidden * up * sig * (1.0 + gate * (1.0 - sig))
    d_up = d_hidden * act
    grad_gate_up = jnp.concatenate([d_gate, d_up], -1).astype(jnp.bfloat16)
    return (grad_gate_up, route_grad, grad_down)


def solution(mesh):
    return jax.shard_map(
        local,
        mesh=mesh,
        in_specs=(
            P(("dp", "expert"), None),
            P(("dp", "expert"), None, None),
            P(("dp", "expert"), None),
            P(("dp", "expert"), None),
            P("expert", "dp", None),
        ),
        out_specs=(
            P(("dp", "expert"), None, None),
            P(("dp", "expert"), None),
            P("expert", "dp", None),
        ),
        check_vma=False,
    )
```

```python
import jax
import jax.numpy as jnp
from jax import lax
from jax.experimental import pallas as pl
from jax.experimental.pallas import tpu as pltpu
from jax.sharding import PartitionSpec as P

MESH = pl.DeviceIdType.MESH


def ring_dp(pos, replicas):
    pos = lax.rem(pos + 2 * replicas, replicas)
    z = pos // 2
    core = lax.rem(pos, 2)
    core = jnp.where(lax.rem(z, 2) == 0, core, 1 - core)
    return z * 2 + core


def ring_pos(dp):
    z = dp // 2
    core = lax.rem(dp, 2)
    return z * 2 + jnp.where(lax.rem(z, 2) == 0, core, 1 - core)


def exchange_kernel(replicas, owners, pieces, w_ref, h_ref, t_ref, o_ref, g_ref, u_ref, sems, send_sem,
                    recv_sem, h_send_sem, h_recv_sem, t_send_sem, t_recv_sem):
    me = lax.axis_index("dp")
    col = lax.axis_index("expert")
    pos = ring_pos(me)
    right = ring_dp(pos + 1, replicas)
    left = ring_dp(pos - 1, replicas)
    cols = w_ref.shape[2] // pieces

    barrier = pltpu.get_barrier_semaphore()
    for neighbour in (left, right):
        pl.semaphore_signal(barrier, inc=1, device_id=(neighbour, col), device_id_type=MESH)
    for peer in range(owners - 1):
        other = lax.rem(col + 1 + peer, owners)
        pl.semaphore_signal(barrier, inc=1, device_id=(me, other), device_id_type=MESH)
    pl.semaphore_wait(barrier, 2 + owners - 1)

    own = pltpu.make_async_copy(w_ref, o_ref.at[:, me], sems.at[0])
    own.start()
    own_h = pltpu.make_async_copy(h_ref.at[col], g_ref.at[col], sems.at[1])
    own_h.start()
    own_t = pltpu.make_async_copy(t_ref.at[col], u_ref.at[col], sems.at[2])
    own_t.start()
    outgoing = []
    for peer in range(owners - 1):
        other = lax.rem(col + 1 + peer, owners)
        for src, dst, ssem, rsem in ((h_ref, g_ref, h_send_sem, h_recv_sem), (t_ref, u_ref, t_send_sem, t_recv_sem)):
            copy = pltpu.make_async_remote_copy(
                src_ref=src.at[other],
                dst_ref=dst.at[col],
                send_sem=ssem.at[other],
                recv_sem=rsem.at[col],
                device_id=(me, other),
                device_id_type=MESH,
            )
            copy.start()
            outgoing.append(copy)

    hops = (replicas // 2, replicas - 1 - replicas // 2)
    for step in range(hops[0]):
        copies = []
        for way, (target, sign) in enumerate(((right, -1), (left, 1))):
            if step >= hops[way]:
                continue
            block = ring_dp(pos + sign * step, replicas)
            for piece in range(pieces):
                part = pl.ds(piece * cols, cols)
                src = w_ref.at[:, :, part] if step == 0 else o_ref.at[:, block, :, part]
                copy = pltpu.make_async_remote_copy(
                    src_ref=src,
                    dst_ref=o_ref.at[:, block, :, part],
                    send_sem=send_sem.at[way, step, piece],
                    recv_sem=recv_sem.at[way, step, piece],
                    device_id=(target, col),
                    device_id_type=MESH,
                )
                copy.start()
                copies.append(copy)
        for copy in copies:
            copy.wait()

    for copy in outgoing:
        copy.wait_send()
    for peer in range(owners - 1):
        source = lax.rem(col + 1 + peer, owners)
        for src, dst, ssem, rsem in ((h_ref, g_ref, h_send_sem, h_recv_sem), (t_ref, u_ref, t_send_sem, t_recv_sem)):
            incoming = pltpu.make_async_remote_copy(
                src_ref=src.at[source],
                dst_ref=dst.at[source],
                send_sem=ssem.at[source],
                recv_sem=rsem.at[source],
                device_id=(me, source),
                device_id_type=MESH,
            )
            incoming.wait_recv()
    own.wait()
    own_h.wait()
    own_t.wait()


def exchange(w_down, h_send, t_send, replicas, owners, pieces=4):
    local_experts, rows, width = w_down.shape
    return pl.pallas_call(
        lambda *refs: exchange_kernel(replicas, owners, pieces, *refs),
        out_shape=(
            jax.ShapeDtypeStruct((local_experts, replicas, rows, width), w_down.dtype),
            jax.ShapeDtypeStruct(h_send.shape, h_send.dtype),
            jax.ShapeDtypeStruct(t_send.shape, t_send.dtype),
        ),
        in_specs=[pl.BlockSpec(memory_space=pl.ANY)] * 3,
        out_specs=(pl.BlockSpec(memory_space=pl.ANY),) * 3,
        scratch_shapes=[
            pltpu.SemaphoreType.DMA((3,)),
            pltpu.SemaphoreType.DMA((2, replicas // 2, pieces)),
            pltpu.SemaphoreType.DMA((2, replicas // 2, pieces)),
            pltpu.SemaphoreType.DMA((owners,)),
            pltpu.SemaphoreType.DMA((owners,)),
            pltpu.SemaphoreType.DMA((owners,)),
            pltpu.SemaphoreType.DMA((owners,)),
        ],
        compiler_params=pltpu.CompilerParams(collective_id=0, has_side_effects=True),
        cost_estimate=pl.CostEstimate(
            flops=0,
            bytes_accessed=2 * replicas * w_down.size * 2 + 2 * h_send.size * 2,
            transcendentals=0,
        ),
    )(w_down, h_send, t_send)


def return_kernel(owners, dy_ref, w_ref, back_ref, gbuf, own_sem, send_sem, recv_sem):
    me = lax.axis_index("dp")
    col = lax.axis_index("expert")
    local_experts = w_ref.shape[0]

    barrier = pltpu.get_barrier_semaphore()
    for peer in range(owners - 1):
        other = lax.rem(col + 1 + peer, owners)
        pl.semaphore_signal(barrier, inc=1, device_id=(me, other), device_id_type=MESH)
    pl.semaphore_wait(barrier, owners - 1)

    def send(source, j):
        return pltpu.make_async_remote_copy(
            src_ref=gbuf.at[source, j],
            dst_ref=back_ref.at[col, j],
            send_sem=send_sem.at[source, j],
            recv_sem=recv_sem.at[col, j],
            device_id=(me, source),
            device_id_type=MESH,
        )

    def step(i, carry):
        source = lax.rem(col + 1 + i, owners)
        for j in range(local_experts):
            gbuf[source, j] = lax.dot_general(
                dy_ref[source, j], w_ref[j], (((1,), (1,)), ((), ())),
                preferred_element_type=jnp.float32,
            ).astype(gbuf.dtype)

        @pl.when(i > 0)
        def _():
            previous = lax.rem(col + i, owners)
            for j in range(local_experts):
                send(previous, j).start()

        return carry

    lax.fori_loop(0, owners, step, 0)
    own = pltpu.make_async_copy(gbuf.at[col], back_ref.at[col], own_sem)
    own.start()

    def finish(peer, carry):
        other = lax.rem(col + 1 + peer, owners)
        for j in range(local_experts):
            send(other, j).wait_send()
        for j in range(local_experts):
            pltpu.make_async_remote_copy(
                src_ref=gbuf.at[other, j],
                dst_ref=back_ref.at[other, j],
                send_sem=send_sem.at[other, j],
                recv_sem=recv_sem.at[other, j],
                device_id=(me, other),
                device_id_type=MESH,
            ).wait_recv()
        return carry

    lax.fori_loop(0, owners - 1, finish, 0)
    own.wait()


def give_back(dy, full_down, owners):
    sources, local_experts, capacity, width = dy.shape
    hidden_units = full_down.shape[1]
    shape = (sources, local_experts, capacity, hidden_units)
    return pl.pallas_call(
        lambda *refs: return_kernel(owners, *refs),
        out_shape=jax.ShapeDtypeStruct(shape, dy.dtype),
        in_specs=[pl.BlockSpec(memory_space=pltpu.VMEM)] * 2,
        out_specs=pl.BlockSpec(memory_space=pl.ANY),
        scratch_shapes=[
            pltpu.VMEM(shape, dy.dtype),
            pltpu.SemaphoreType.DMA(()),
            pltpu.SemaphoreType.DMA((owners, local_experts)),
            pltpu.SemaphoreType.DMA((owners, local_experts)),
        ],
        compiler_params=pltpu.CompilerParams(
            collective_id=1, has_side_effects=True, vmem_limit_bytes=48 * 1024 * 1024
        ),
        cost_estimate=pl.CostEstimate(
            flops=2 * sources * local_experts * capacity * width * hidden_units,
            bytes_accessed=(dy.size + full_down.size + 2 * sources * local_experts * capacity * hidden_units) * 2,
            transcendentals=0,
        ),
    )(dy, full_down)


def slot_counts(ids, experts):
    routes = ids.shape[-1]
    onehot = (ids[..., None] == jnp.arange(experts, dtype=jnp.int32)).astype(jnp.bfloat16)
    lower = (jnp.arange(routes)[:, None] > jnp.arange(routes)[None, :]).astype(jnp.bfloat16)
    before = jnp.einsum("rq,...qe->...re", lower, onehot, preferred_element_type=jnp.float32)
    return jnp.sum(before * onehot.astype(jnp.float32), axis=-1).astype(jnp.int32)


def local(cotangent, saved_gate_up, route_ids, route_weights, w_down):
    tokens, top = route_ids.shape
    width = cotangent.shape[1]
    hidden_units = saved_gate_up.shape[2] // 2
    owners = lax.axis_size("expert")
    replicas = lax.axis_size("dp")
    me = lax.axis_index("expert")
    local_experts = w_down.shape[0]
    experts = local_experts * owners
    capacity = min(tokens, 2 * tokens * top // experts)
    routes = tokens * top

    cot_group = lax.all_gather(cotangent, "expert", axis=0, tiled=True)

    gate = saved_gate_up[:, :, :hidden_units].astype(jnp.float32)
    up = saved_gate_up[:, :, hidden_units:].astype(jnp.float32)
    sig = jax.nn.sigmoid(gate)
    act = gate * sig
    hidden = (act * up).astype(jnp.bfloat16)
    weights = route_weights[:, :, None]
    scaled = (weights * hidden.astype(jnp.float32)).astype(jnp.bfloat16)

    flat_ids = route_ids.reshape(routes)
    slot = slot_counts(flat_ids, experts)
    position = flat_ids * capacity + slot
    slot_ids = jnp.arange(experts * capacity, dtype=jnp.int32)
    match = position[None, :] == slot_ids[:, None]
    route_of_slot = jnp.sum(jnp.where(match, jnp.arange(routes, dtype=jnp.int32)[None, :], 0), axis=1)
    filled = jnp.any(match, axis=1)
    h_rows = jnp.where(filled[:, None], scaled.reshape(routes, hidden_units)[route_of_slot], jnp.zeros((), jnp.bfloat16))
    h_send = h_rows.reshape(owners, local_experts, capacity, hidden_units)

    t_send = jnp.where(filled, route_of_slot // top, -1).reshape(owners, 1, local_experts * capacity)
    full_down, h_got, t_got = exchange(w_down, h_send, t_send, replicas, owners)
    h_got, t_got, cot_group = lax.optimization_barrier((h_got, t_got, cot_group))
    pick = (t_got.reshape(owners, local_experts * capacity, 1)
            == jnp.arange(tokens, dtype=jnp.int32)[None, None, :]).astype(jnp.bfloat16)
    dy = jnp.einsum(
        "sct,std->scd", pick, cot_group.reshape(owners, tokens, width),
        preferred_element_type=jnp.bfloat16,
    ).reshape(owners, local_experts, capacity, width)

    parts = []
    for j in range(local_experts):
        part = jnp.einsum(
            "scf,scd->fd", h_got[:, j], dy[:, j], preferred_element_type=jnp.float32
        ).astype(jnp.bfloat16)
        parts.append(part.reshape(replicas, hidden_units // replicas, width))
    stacked = jnp.stack(parts, axis=1)
    stacked, dy = lax.optimization_barrier((stacked, dy))
    summed = lax.psum_scatter(stacked, "dp", scatter_dimension=0, tiled=True)
    grad_down = summed[0].astype(jnp.float32)
    back = give_back(dy, full_down.reshape(local_experts, hidden_units, width), owners)
    take = (position[:, None] == jnp.arange(experts * capacity, dtype=jnp.int32)[None, :]).astype(jnp.bfloat16)
    rows = jnp.dot(take, back.reshape(experts * capacity, hidden_units), preferred_element_type=jnp.bfloat16)
    qf = lax.optimization_barrier(rows).reshape(tokens, top, hidden_units).astype(jnp.float32)
    route_grad = jnp.sum(qf * hidden.astype(jnp.float32), -1)
    d_hidden = weights * qf
    d_gate = d_hidden * up * sig * (1.0 + gate * (1.0 - sig))
    d_up = d_hidden * act
    grad_gate_up = jnp.concatenate([d_gate, d_up], -1).astype(jnp.bfloat16)
    return (grad_gate_up, route_grad, grad_down)


def solution(mesh):
    return jax.shard_map(
        local,
        mesh=mesh,
        in_specs=(
            P(("dp", "expert"), None),
            P(("dp", "expert"), None, None),
            P(("dp", "expert"), None),
            P(("dp", "expert"), None),
            P("expert", "dp", None),
        ),
        out_specs=(
            P(("dp", "expert"), None, None),
            P(("dp", "expert"), None),
            P("expert", "dp", None),
        ),
        check_vma=False,
    )
```

```python
import jax
import jax.numpy as jnp
from jax import lax
from jax.experimental import pallas as pl
from jax.experimental.pallas import tpu as pltpu
from jax.sharding import PartitionSpec as P

MESH = pl.DeviceIdType.MESH


def ring_dp(pos, replicas):
    pos = lax.rem(pos + 2 * replicas, replicas)
    z = pos // 2
    core = lax.rem(pos, 2)
    core = jnp.where(lax.rem(z, 2) == 0, core, 1 - core)
    return z * 2 + core


def ring_pos(dp):
    z = dp // 2
    core = lax.rem(dp, 2)
    return z * 2 + jnp.where(lax.rem(z, 2) == 0, core, 1 - core)


def exchange_kernel(replicas, owners, pieces, w_ref, h_ref, t_ref, o_ref, g_ref, u_ref, sems, send_sem,
                    recv_sem, h_send_sem, h_recv_sem, t_send_sem, t_recv_sem):
    me = lax.axis_index("dp")
    col = lax.axis_index("expert")
    pos = ring_pos(me)
    right = ring_dp(pos + 1, replicas)
    left = ring_dp(pos - 1, replicas)
    cols = w_ref.shape[2] // pieces

    barrier = pltpu.get_barrier_semaphore()
    for neighbour in (left, right):
        pl.semaphore_signal(barrier, inc=1, device_id=(neighbour, col), device_id_type=MESH)
    for peer in range(owners - 1):
        other = lax.rem(col + 1 + peer, owners)
        pl.semaphore_signal(barrier, inc=1, device_id=(me, other), device_id_type=MESH)
    pl.semaphore_wait(barrier, 2 + owners - 1)

    own = pltpu.make_async_copy(w_ref, o_ref.at[:, me], sems.at[0])
    own.start()
    own_h = pltpu.make_async_copy(h_ref.at[col], g_ref.at[col], sems.at[1])
    own_h.start()
    own_t = pltpu.make_async_copy(t_ref.at[col], u_ref.at[col], sems.at[2])
    own_t.start()
    outgoing = []
    for peer in range(owners - 1):
        other = lax.rem(col + 1 + peer, owners)
        for src, dst, ssem, rsem in ((h_ref, g_ref, h_send_sem, h_recv_sem), (t_ref, u_ref, t_send_sem, t_recv_sem)):
            copy = pltpu.make_async_remote_copy(
                src_ref=src.at[other],
                dst_ref=dst.at[col],
                send_sem=ssem.at[other],
                recv_sem=rsem.at[col],
                device_id=(me, other),
                device_id_type=MESH,
            )
            copy.start()
            outgoing.append(copy)

    hops = (replicas // 2, replicas - 1 - replicas // 2)
    for step in range(hops[0]):
        copies = []
        for way, (target, sign) in enumerate(((right, -1), (left, 1))):
            if step >= hops[way]:
                continue
            block = ring_dp(pos + sign * step, replicas)
            for piece in range(pieces):
                part = pl.ds(piece * cols, cols)
                src = w_ref.at[:, :, part] if step == 0 else o_ref.at[:, block, :, part]
                copy = pltpu.make_async_remote_copy(
                    src_ref=src,
                    dst_ref=o_ref.at[:, block, :, part],
                    send_sem=send_sem.at[way, step, piece],
                    recv_sem=recv_sem.at[way, step, piece],
                    device_id=(target, col),
                    device_id_type=MESH,
                )
                copy.start()
                copies.append(copy)
        for copy in copies:
            copy.wait()

    for copy in outgoing:
        copy.wait_send()
    for peer in range(owners - 1):
        source = lax.rem(col + 1 + peer, owners)
        for src, dst, ssem, rsem in ((h_ref, g_ref, h_send_sem, h_recv_sem), (t_ref, u_ref, t_send_sem, t_recv_sem)):
            incoming = pltpu.make_async_remote_copy(
                src_ref=src.at[source],
                dst_ref=dst.at[source],
                send_sem=ssem.at[source],
                recv_sem=rsem.at[source],
                device_id=(me, source),
                device_id_type=MESH,
            )
            incoming.wait_recv()
    own.wait()
    own_h.wait()
    own_t.wait()


def exchange(w_down, h_send, t_send, replicas, owners, pieces=4):
    local_experts, rows, width = w_down.shape
    return pl.pallas_call(
        lambda *refs: exchange_kernel(replicas, owners, pieces, *refs),
        out_shape=(
            jax.ShapeDtypeStruct((local_experts, replicas, rows, width), w_down.dtype),
            jax.ShapeDtypeStruct(h_send.shape, h_send.dtype),
            jax.ShapeDtypeStruct(t_send.shape, t_send.dtype),
        ),
        in_specs=[pl.BlockSpec(memory_space=pl.ANY)] * 3,
        out_specs=(pl.BlockSpec(memory_space=pl.ANY),) * 3,
        scratch_shapes=[
            pltpu.SemaphoreType.DMA((3,)),
            pltpu.SemaphoreType.DMA((2, replicas // 2, pieces)),
            pltpu.SemaphoreType.DMA((2, replicas // 2, pieces)),
            pltpu.SemaphoreType.DMA((owners,)),
            pltpu.SemaphoreType.DMA((owners,)),
            pltpu.SemaphoreType.DMA((owners,)),
            pltpu.SemaphoreType.DMA((owners,)),
        ],
        compiler_params=pltpu.CompilerParams(collective_id=0, has_side_effects=True),
        cost_estimate=pl.CostEstimate(
            flops=0,
            bytes_accessed=2 * replicas * w_down.size * 2 + 2 * h_send.size * 2,
            transcendentals=0,
        ),
    )(w_down, h_send, t_send)


def return_kernel(owners, dy_ref, w_ref, back_ref, gbuf, own_sem, send_sem, recv_sem):
    me = lax.axis_index("dp")
    col = lax.axis_index("expert")
    local_experts = w_ref.shape[0]

    def grads_of(source):
        for j in range(local_experts):
            gbuf[source, j] = lax.dot_general(
                dy_ref[source, j], w_ref[j], (((1,), (1,)), ((), ())),
                preferred_element_type=jnp.float32,
            ).astype(gbuf.dtype)

    grads_of(lax.rem(col + 1, owners))
    barrier = pltpu.get_barrier_semaphore()
    for peer in range(owners - 1):
        other = lax.rem(col + 1 + peer, owners)
        pl.semaphore_signal(barrier, inc=1, device_id=(me, other), device_id_type=MESH)
    pl.semaphore_wait(barrier, owners - 1)

    def send(source, j):
        return pltpu.make_async_remote_copy(
            src_ref=gbuf.at[source, j],
            dst_ref=back_ref.at[col, j],
            send_sem=send_sem.at[source, j],
            recv_sem=recv_sem.at[col, j],
            device_id=(me, source),
            device_id_type=MESH,
        )

    def step(i, carry):
        grads_of(lax.rem(col + 1 + i, owners))
        previous = lax.rem(col + i, owners)
        for j in range(local_experts):
            send(previous, j).start()
        return carry

    lax.fori_loop(1, owners, step, 0)
    own = pltpu.make_async_copy(gbuf.at[col], back_ref.at[col], own_sem)
    own.start()

    def finish(peer, carry):
        other = lax.rem(col + 1 + peer, owners)
        for j in range(local_experts):
            send(other, j).wait_send()
        for j in range(local_experts):
            pltpu.make_async_remote_copy(
                src_ref=gbuf.at[other, j],
                dst_ref=back_ref.at[other, j],
                send_sem=send_sem.at[other, j],
                recv_sem=recv_sem.at[other, j],
                device_id=(me, other),
                device_id_type=MESH,
            ).wait_recv()
        return carry

    lax.fori_loop(0, owners - 1, finish, 0)
    own.wait()


def give_back(dy, full_down, owners):
    sources, local_experts, capacity, width = dy.shape
    hidden_units = full_down.shape[1]
    shape = (sources, local_experts, capacity, hidden_units)
    return pl.pallas_call(
        lambda *refs: return_kernel(owners, *refs),
        out_shape=jax.ShapeDtypeStruct(shape, dy.dtype),
        in_specs=[pl.BlockSpec(memory_space=pltpu.VMEM)] * 2,
        out_specs=pl.BlockSpec(memory_space=pl.ANY),
        scratch_shapes=[
            pltpu.VMEM(shape, dy.dtype),
            pltpu.SemaphoreType.DMA(()),
            pltpu.SemaphoreType.DMA((owners, local_experts)),
            pltpu.SemaphoreType.DMA((owners, local_experts)),
        ],
        compiler_params=pltpu.CompilerParams(
            collective_id=1, has_side_effects=True, vmem_limit_bytes=48 * 1024 * 1024
        ),
        cost_estimate=pl.CostEstimate(
            flops=2 * sources * local_experts * capacity * width * hidden_units,
            bytes_accessed=(dy.size + full_down.size + 2 * sources * local_experts * capacity * hidden_units) * 2,
            transcendentals=0,
        ),
    )(dy, full_down)


def slot_counts(ids, experts):
    routes = ids.shape[-1]
    onehot = (ids[..., None] == jnp.arange(experts, dtype=jnp.int32)).astype(jnp.bfloat16)
    lower = (jnp.arange(routes)[:, None] > jnp.arange(routes)[None, :]).astype(jnp.bfloat16)
    before = jnp.einsum("rq,...qe->...re", lower, onehot, preferred_element_type=jnp.float32)
    return jnp.sum(before * onehot.astype(jnp.float32), axis=-1).astype(jnp.int32)


def local(cotangent, saved_gate_up, route_ids, route_weights, w_down):
    tokens, top = route_ids.shape
    width = cotangent.shape[1]
    hidden_units = saved_gate_up.shape[2] // 2
    owners = lax.axis_size("expert")
    replicas = lax.axis_size("dp")
    me = lax.axis_index("expert")
    local_experts = w_down.shape[0]
    experts = local_experts * owners
    capacity = min(tokens, 2 * tokens * top // experts)
    routes = tokens * top

    cot_group = lax.all_gather(cotangent, "expert", axis=0, tiled=True)

    gate = saved_gate_up[:, :, :hidden_units].astype(jnp.float32)
    up = saved_gate_up[:, :, hidden_units:].astype(jnp.float32)
    sig = jax.nn.sigmoid(gate)
    act = gate * sig
    hidden = (act * up).astype(jnp.bfloat16)
    weights = route_weights[:, :, None]
    scaled = (weights * hidden.astype(jnp.float32)).astype(jnp.bfloat16)

    flat_ids = route_ids.reshape(routes)
    slot = slot_counts(flat_ids, experts)
    position = flat_ids * capacity + slot
    slot_ids = jnp.arange(experts * capacity, dtype=jnp.int32)
    match = position[None, :] == slot_ids[:, None]
    route_of_slot = jnp.sum(jnp.where(match, jnp.arange(routes, dtype=jnp.int32)[None, :], 0), axis=1)
    filled = jnp.any(match, axis=1)
    h_rows = jnp.where(filled[:, None], scaled.reshape(routes, hidden_units)[route_of_slot], jnp.zeros((), jnp.bfloat16))
    h_send = h_rows.reshape(owners, local_experts, capacity, hidden_units)

    t_send = jnp.where(filled, route_of_slot // top, -1).reshape(owners, 1, local_experts * capacity)
    full_down, h_got, t_got = exchange(w_down, h_send, t_send, replicas, owners)
    h_got, t_got, cot_group = lax.optimization_barrier((h_got, t_got, cot_group))
    pick = (t_got.reshape(owners, local_experts * capacity, 1)
            == jnp.arange(tokens, dtype=jnp.int32)[None, None, :]).astype(jnp.bfloat16)
    dy = jnp.einsum(
        "sct,std->scd", pick, cot_group.reshape(owners, tokens, width),
        preferred_element_type=jnp.bfloat16,
    ).reshape(owners, local_experts, capacity, width)

    parts = []
    for j in range(local_experts):
        part = jnp.einsum(
            "scf,scd->fd", h_got[:, j], dy[:, j], preferred_element_type=jnp.float32
        ).astype(jnp.bfloat16)
        parts.append(part.reshape(replicas, hidden_units // replicas, width))
    stacked = jnp.stack(parts, axis=1)
    stacked, dy = lax.optimization_barrier((stacked, dy))
    summed = lax.psum_scatter(stacked, "dp", scatter_dimension=0, tiled=True)
    grad_down = summed[0].astype(jnp.float32)
    back = give_back(dy, full_down.reshape(local_experts, hidden_units, width), owners)
    take = (position.reshape(tokens, top, 1)
            == jnp.arange(experts * capacity, dtype=jnp.int32)[None, None, :]).astype(jnp.bfloat16)
    qf = jnp.einsum(
        "tkr,rf->tkf", take, back.reshape(experts * capacity, hidden_units),
        preferred_element_type=jnp.float32,
    )
    route_grad = jnp.sum(qf * hidden.astype(jnp.float32), -1)
    d_hidden = weights * qf
    d_gate = d_hidden * up * sig * (1.0 + gate * (1.0 - sig))
    d_up = d_hidden * act
    grad_gate_up = jnp.concatenate([d_gate, d_up], -1).astype(jnp.bfloat16)
    return (grad_gate_up, route_grad, grad_down)


def solution(mesh):
    return jax.shard_map(
        local,
        mesh=mesh,
        in_specs=(
            P(("dp", "expert"), None),
            P(("dp", "expert"), None, None),
            P(("dp", "expert"), None),
            P(("dp", "expert"), None),
            P("expert", "dp", None),
        ),
        out_specs=(
            P(("dp", "expert"), None, None),
            P(("dp", "expert"), None),
            P("expert", "dp", None),
        ),
        check_vma=False,
    )
```

```python
import jax
import jax.numpy as jnp
from jax import lax
from jax.experimental import pallas as pl
from jax.experimental.pallas import tpu as pltpu
from jax.sharding import PartitionSpec as P

MESH = pl.DeviceIdType.MESH


def ring_dp(pos, replicas):
    pos = lax.rem(pos + 2 * replicas, replicas)
    z = pos // 2
    core = lax.rem(pos, 2)
    core = jnp.where(lax.rem(z, 2) == 0, core, 1 - core)
    return z * 2 + core


def ring_pos(dp):
    z = dp // 2
    core = lax.rem(dp, 2)
    return z * 2 + jnp.where(lax.rem(z, 2) == 0, core, 1 - core)


def exchange_kernel(replicas, owners, pieces, w_ref, h_ref, t_ref, o_ref, g_ref, u_ref, sems, send_sem,
                    recv_sem, h_send_sem, h_recv_sem, t_send_sem, t_recv_sem):
    me = lax.axis_index("dp")
    col = lax.axis_index("expert")
    pos = ring_pos(me)
    right = ring_dp(pos + 1, replicas)
    left = ring_dp(pos - 1, replicas)
    cols = w_ref.shape[2] // pieces

    barrier = pltpu.get_barrier_semaphore()
    for neighbour in (left, right):
        pl.semaphore_signal(barrier, inc=1, device_id=(neighbour, col), device_id_type=MESH)
    for peer in range(owners - 1):
        other = lax.rem(col + 1 + peer, owners)
        pl.semaphore_signal(barrier, inc=1, device_id=(me, other), device_id_type=MESH)
    pl.semaphore_wait(barrier, 2 + owners - 1)

    own = pltpu.make_async_copy(w_ref, o_ref.at[:, me], sems.at[0])
    own.start()
    own_h = pltpu.make_async_copy(h_ref.at[col], g_ref.at[col], sems.at[1])
    own_h.start()
    own_t = pltpu.make_async_copy(t_ref.at[col], u_ref.at[col], sems.at[2])
    own_t.start()
    outgoing = []
    for peer in range(owners - 1):
        other = lax.rem(col + 1 + peer, owners)
        for src, dst, ssem, rsem in ((h_ref, g_ref, h_send_sem, h_recv_sem), (t_ref, u_ref, t_send_sem, t_recv_sem)):
            copy = pltpu.make_async_remote_copy(
                src_ref=src.at[other],
                dst_ref=dst.at[col],
                send_sem=ssem.at[other],
                recv_sem=rsem.at[col],
                device_id=(me, other),
                device_id_type=MESH,
            )
            copy.start()
            outgoing.append(copy)

    hops = (replicas // 2, replicas - 1 - replicas // 2)
    for step in range(hops[0]):
        copies = []
        for way, (target, sign) in enumerate(((right, -1), (left, 1))):
            if step >= hops[way]:
                continue
            block = ring_dp(pos + sign * step, replicas)
            for piece in range(pieces):
                part = pl.ds(piece * cols, cols)
                src = w_ref.at[:, :, part] if step == 0 else o_ref.at[:, block, :, part]
                copy = pltpu.make_async_remote_copy(
                    src_ref=src,
                    dst_ref=o_ref.at[:, block, :, part],
                    send_sem=send_sem.at[way, step, piece],
                    recv_sem=recv_sem.at[way, step, piece],
                    device_id=(target, col),
                    device_id_type=MESH,
                )
                copy.start()
                copies.append(copy)
        for copy in copies:
            copy.wait()

    for copy in outgoing:
        copy.wait_send()
    for peer in range(owners - 1):
        source = lax.rem(col + 1 + peer, owners)
        for src, dst, ssem, rsem in ((h_ref, g_ref, h_send_sem, h_recv_sem), (t_ref, u_ref, t_send_sem, t_recv_sem)):
            incoming = pltpu.make_async_remote_copy(
                src_ref=src.at[source],
                dst_ref=dst.at[source],
                send_sem=ssem.at[source],
                recv_sem=rsem.at[source],
                device_id=(me, source),
                device_id_type=MESH,
            )
            incoming.wait_recv()
    own.wait()
    own_h.wait()
    own_t.wait()


def exchange(w_down, h_send, t_send, replicas, owners, pieces=4):
    local_experts, rows, width = w_down.shape
    return pl.pallas_call(
        lambda *refs: exchange_kernel(replicas, owners, pieces, *refs),
        out_shape=(
            jax.ShapeDtypeStruct((local_experts, replicas, rows, width), w_down.dtype),
            jax.ShapeDtypeStruct(h_send.shape, h_send.dtype),
            jax.ShapeDtypeStruct(t_send.shape, t_send.dtype),
        ),
        in_specs=[pl.BlockSpec(memory_space=pl.ANY)] * 3,
        out_specs=(pl.BlockSpec(memory_space=pl.ANY),) * 3,
        scratch_shapes=[
            pltpu.SemaphoreType.DMA((3,)),
            pltpu.SemaphoreType.DMA((2, replicas // 2, pieces)),
            pltpu.SemaphoreType.DMA((2, replicas // 2, pieces)),
            pltpu.SemaphoreType.DMA((owners,)),
            pltpu.SemaphoreType.DMA((owners,)),
            pltpu.SemaphoreType.DMA((owners,)),
            pltpu.SemaphoreType.DMA((owners,)),
        ],
        compiler_params=pltpu.CompilerParams(collective_id=0, has_side_effects=True),
        cost_estimate=pl.CostEstimate(
            flops=0,
            bytes_accessed=2 * replicas * w_down.size * 2 + 2 * h_send.size * 2,
            transcendentals=0,
        ),
    )(w_down, h_send, t_send)


def return_kernel(owners, dy_ref, w_ref, back_ref, gbuf, own_sem, send_sem, recv_sem):
    me = lax.axis_index("dp")
    col = lax.axis_index("expert")
    local_experts = w_ref.shape[0]

    def grads_of(source):
        for j in range(local_experts):
            gbuf[source, j] = lax.dot_general(
                dy_ref[source, j], w_ref[j], (((1,), (1,)), ((), ())),
                preferred_element_type=jnp.float32,
            ).astype(gbuf.dtype)

    grads_of(lax.rem(col + 1, owners))
    barrier = pltpu.get_barrier_semaphore()
    for peer in range(owners - 1):
        other = lax.rem(col + 1 + peer, owners)
        pl.semaphore_signal(barrier, inc=1, device_id=(me, other), device_id_type=MESH)
    pl.semaphore_wait(barrier, owners - 1)

    def send(source, j):
        return pltpu.make_async_remote_copy(
            src_ref=gbuf.at[source, j],
            dst_ref=back_ref.at[col, j],
            send_sem=send_sem.at[source, j],
            recv_sem=recv_sem.at[col, j],
            device_id=(me, source),
            device_id_type=MESH,
        )

    def step(i, carry):
        grads_of(lax.rem(col + 1 + i, owners))
        previous = lax.rem(col + i, owners)
        for j in range(local_experts):
            send(previous, j).start()
        return carry

    lax.fori_loop(1, owners, step, 0)
    own = pltpu.make_async_copy(gbuf.at[col], back_ref.at[col], own_sem)
    own.start()

    def finish(peer, carry):
        other = lax.rem(col + 1 + peer, owners)
        for j in range(local_experts):
            send(other, j).wait_send()
        for j in range(local_experts):
            pltpu.make_async_remote_copy(
                src_ref=gbuf.at[other, j],
                dst_ref=back_ref.at[other, j],
                send_sem=send_sem.at[other, j],
                recv_sem=recv_sem.at[other, j],
                device_id=(me, other),
                device_id_type=MESH,
            ).wait_recv()
        return carry

    lax.fori_loop(0, owners - 1, finish, 0)
    own.wait()


def give_back(dy, full_down, owners):
    sources, local_experts, capacity, width = dy.shape
    hidden_units = full_down.shape[1]
    shape = (sources, local_experts, capacity, hidden_units)
    return pl.pallas_call(
        lambda *refs: return_kernel(owners, *refs),
        out_shape=jax.ShapeDtypeStruct(shape, dy.dtype),
        in_specs=[pl.BlockSpec(memory_space=pltpu.VMEM)] * 2,
        out_specs=pl.BlockSpec(memory_space=pl.ANY),
        scratch_shapes=[
            pltpu.VMEM(shape, dy.dtype),
            pltpu.SemaphoreType.DMA(()),
            pltpu.SemaphoreType.DMA((owners, local_experts)),
            pltpu.SemaphoreType.DMA((owners, local_experts)),
        ],
        compiler_params=pltpu.CompilerParams(
            collective_id=1, has_side_effects=True, vmem_limit_bytes=48 * 1024 * 1024
        ),
        cost_estimate=pl.CostEstimate(
            flops=2 * sources * local_experts * capacity * width * hidden_units,
            bytes_accessed=(dy.size + full_down.size + 2 * sources * local_experts * capacity * hidden_units) * 2,
            transcendentals=0,
        ),
    )(dy, full_down)


def slot_counts(ids, experts):
    routes = ids.shape[-1]
    onehot = (ids[..., None] == jnp.arange(experts, dtype=jnp.int32)).astype(jnp.bfloat16)
    lower = (jnp.arange(routes)[:, None] > jnp.arange(routes)[None, :]).astype(jnp.bfloat16)
    before = jnp.einsum("rq,...qe->...re", lower, onehot, preferred_element_type=jnp.float32)
    return jnp.sum(before * onehot.astype(jnp.float32), axis=-1).astype(jnp.int32)


def local(cotangent, saved_gate_up, route_ids, route_weights, w_down):
    tokens, top = route_ids.shape
    width = cotangent.shape[1]
    hidden_units = saved_gate_up.shape[2] // 2
    owners = lax.axis_size("expert")
    replicas = lax.axis_size("dp")
    me = lax.axis_index("expert")
    local_experts = w_down.shape[0]
    experts = local_experts * owners
    capacity = min(tokens, 2 * tokens * top // experts)
    routes = tokens * top

    cot_group = lax.all_gather(cotangent, "expert", axis=0, tiled=True)

    gate = saved_gate_up[:, :, :hidden_units].astype(jnp.float32)
    up = saved_gate_up[:, :, hidden_units:].astype(jnp.float32)
    sig = jax.nn.sigmoid(gate)
    act = gate * sig
    hidden = (act * up).astype(jnp.bfloat16)
    weights = route_weights[:, :, None]
    scaled = (weights * hidden.astype(jnp.float32)).astype(jnp.bfloat16)

    flat_ids = route_ids.reshape(routes)
    slot = slot_counts(flat_ids, experts)
    position = flat_ids * capacity + slot
    slot_ids = jnp.arange(experts * capacity, dtype=jnp.int32)
    match = position[None, :] == slot_ids[:, None]
    route_of_slot = jnp.sum(jnp.where(match, jnp.arange(routes, dtype=jnp.int32)[None, :], 0), axis=1)
    filled = jnp.any(match, axis=1)
    h_rows = jnp.where(filled[:, None], scaled.reshape(routes, hidden_units)[route_of_slot], jnp.zeros((), jnp.bfloat16))
    h_send = h_rows.reshape(owners, local_experts, capacity, hidden_units)

    t_send = jnp.where(filled, route_of_slot // top, -1).reshape(owners, 1, local_experts * capacity)
    full_down, h_got, t_got = exchange(w_down, h_send, t_send, replicas, owners)
    h_got, t_got, cot_group = lax.optimization_barrier((h_got, t_got, cot_group))
    pick = (t_got.reshape(owners, local_experts * capacity, 1)
            == jnp.arange(tokens, dtype=jnp.int32)[None, None, :]).astype(jnp.bfloat16)
    dy = jnp.einsum(
        "sct,std->scd", pick, cot_group.reshape(owners, tokens, width),
        preferred_element_type=jnp.bfloat16,
    ).reshape(owners, local_experts, capacity, width)

    parts = []
    for j in range(local_experts):
        part = jnp.einsum(
            "scf,scd->fd", h_got[:, j], dy[:, j], preferred_element_type=jnp.float32
        ).astype(jnp.bfloat16)
        parts.append(part.reshape(replicas, hidden_units // replicas, width))
    stacked = jnp.stack(parts, axis=1)
    stacked, dy = lax.optimization_barrier((stacked, dy))
    summed = lax.psum_scatter(stacked, "dp", scatter_dimension=0, tiled=True)
    grad_down = summed[0].astype(jnp.float32)
    back = give_back(dy, full_down.reshape(local_experts, hidden_units, width), owners)
    take = (position[:, None] == jnp.arange(experts * capacity, dtype=jnp.int32)[None, :]).astype(jnp.bfloat16)
    rows = jnp.dot(take, back.reshape(experts * capacity, hidden_units), preferred_element_type=jnp.bfloat16)
    qf = lax.optimization_barrier(rows).reshape(tokens, top, hidden_units).astype(jnp.float32)
    route_grad = jnp.sum(qf * hidden.astype(jnp.float32), -1)
    d_hidden = weights * qf
    d_gate = d_hidden * up * sig * (1.0 + gate * (1.0 - sig))
    d_up = d_hidden * act
    grad_gate_up = jnp.concatenate([d_gate, d_up], -1).astype(jnp.bfloat16)
    return (grad_gate_up, route_grad, grad_down)


def solution(mesh):
    return jax.shard_map(
        local,
        mesh=mesh,
        in_specs=(
            P(("dp", "expert"), None),
            P(("dp", "expert"), None, None),
            P(("dp", "expert"), None),
            P(("dp", "expert"), None),
            P("expert", "dp", None),
        ),
        out_specs=(
            P(("dp", "expert"), None, None),
            P(("dp", "expert"), None),
            P("expert", "dp", None),
        ),
        check_vma=False,
    )
```

```python
import jax
import jax.numpy as jnp
from jax import lax
from jax.experimental import pallas as pl
from jax.experimental.pallas import tpu as pltpu
from jax.sharding import PartitionSpec as P

MESH = pl.DeviceIdType.MESH


def ring_dp(pos, replicas):
    pos = lax.rem(pos + 2 * replicas, replicas)
    z = pos // 2
    core = lax.rem(pos, 2)
    core = jnp.where(lax.rem(z, 2) == 0, core, 1 - core)
    return z * 2 + core


def ring_pos(dp):
    z = dp // 2
    core = lax.rem(dp, 2)
    return z * 2 + jnp.where(lax.rem(z, 2) == 0, core, 1 - core)


def exchange_kernel(replicas, owners, pieces, w_ref, h_ref, t_ref, o_ref, g_ref, u_ref, sems, send_sem,
                    recv_sem, h_send_sem, h_recv_sem, t_send_sem, t_recv_sem):
    me = lax.axis_index("dp")
    col = lax.axis_index("expert")
    pos = ring_pos(me)
    right = ring_dp(pos + 1, replicas)
    left = ring_dp(pos - 1, replicas)
    cols = w_ref.shape[2] // pieces

    barrier = pltpu.get_barrier_semaphore()
    for neighbour in (left, right):
        pl.semaphore_signal(barrier, inc=1, device_id=(neighbour, col), device_id_type=MESH)
    for peer in range(owners - 1):
        other = lax.rem(col + 1 + peer, owners)
        pl.semaphore_signal(barrier, inc=1, device_id=(me, other), device_id_type=MESH)
    pl.semaphore_wait(barrier, 2 + owners - 1)

    own = pltpu.make_async_copy(w_ref, o_ref.at[:, me], sems.at[0])
    own.start()
    own_h = pltpu.make_async_copy(h_ref.at[col], g_ref.at[col], sems.at[1])
    own_h.start()
    own_t = pltpu.make_async_copy(t_ref.at[col], u_ref.at[col], sems.at[2])
    own_t.start()
    outgoing = []
    for peer in range(owners - 1):
        other = lax.rem(col + 1 + peer, owners)
        for src, dst, ssem, rsem in ((h_ref, g_ref, h_send_sem, h_recv_sem), (t_ref, u_ref, t_send_sem, t_recv_sem)):
            copy = pltpu.make_async_remote_copy(
                src_ref=src.at[other],
                dst_ref=dst.at[col],
                send_sem=ssem.at[other],
                recv_sem=rsem.at[col],
                device_id=(me, other),
                device_id_type=MESH,
            )
            copy.start()
            outgoing.append(copy)

    hops = (replicas // 2, replicas - 1 - replicas // 2)
    for step in range(hops[0]):
        copies = []
        for way, (target, sign) in enumerate(((right, -1), (left, 1))):
            if step >= hops[way]:
                continue
            block = ring_dp(pos + sign * step, replicas)
            for piece in range(pieces):
                part = pl.ds(piece * cols, cols)
                src = w_ref.at[:, :, part] if step == 0 else o_ref.at[:, block, :, part]
                copy = pltpu.make_async_remote_copy(
                    src_ref=src,
                    dst_ref=o_ref.at[:, block, :, part],
                    send_sem=send_sem.at[way, step, piece],
                    recv_sem=recv_sem.at[way, step, piece],
                    device_id=(target, col),
                    device_id_type=MESH,
                )
                copy.start()
                copies.append(copy)
        for copy in copies:
            copy.wait()

    for copy in outgoing:
        copy.wait_send()
    for peer in range(owners - 1):
        source = lax.rem(col + 1 + peer, owners)
        for src, dst, ssem, rsem in ((h_ref, g_ref, h_send_sem, h_recv_sem), (t_ref, u_ref, t_send_sem, t_recv_sem)):
            incoming = pltpu.make_async_remote_copy(
                src_ref=src.at[source],
                dst_ref=dst.at[source],
                send_sem=ssem.at[source],
                recv_sem=rsem.at[source],
                device_id=(me, source),
                device_id_type=MESH,
            )
            incoming.wait_recv()
    own.wait()
    own_h.wait()
    own_t.wait()


def exchange(w_down, h_send, t_send, replicas, owners, pieces=4):
    local_experts, rows, width = w_down.shape
    return pl.pallas_call(
        lambda *refs: exchange_kernel(replicas, owners, pieces, *refs),
        out_shape=(
            jax.ShapeDtypeStruct((local_experts, replicas, rows, width), w_down.dtype),
            jax.ShapeDtypeStruct(h_send.shape, h_send.dtype),
            jax.ShapeDtypeStruct(t_send.shape, t_send.dtype),
        ),
        in_specs=[pl.BlockSpec(memory_space=pl.ANY)] * 3,
        out_specs=(pl.BlockSpec(memory_space=pl.ANY),) * 3,
        scratch_shapes=[
            pltpu.SemaphoreType.DMA((3,)),
            pltpu.SemaphoreType.DMA((2, replicas // 2, pieces)),
            pltpu.SemaphoreType.DMA((2, replicas // 2, pieces)),
            pltpu.SemaphoreType.DMA((owners,)),
            pltpu.SemaphoreType.DMA((owners,)),
            pltpu.SemaphoreType.DMA((owners,)),
            pltpu.SemaphoreType.DMA((owners,)),
        ],
        compiler_params=pltpu.CompilerParams(collective_id=0, has_side_effects=True),
        cost_estimate=pl.CostEstimate(
            flops=0,
            bytes_accessed=2 * replicas * w_down.size * 2 + 2 * h_send.size * 2,
            transcendentals=0,
        ),
    )(w_down, h_send, t_send)


def return_kernel(owners, dy_ref, w_ref, back_ref, gbuf, own_sem, send_sem, recv_sem):
    me = lax.axis_index("dp")
    col = lax.axis_index("expert")
    local_experts = w_ref.shape[0]

    def grads_of(source):
        for j in range(local_experts):
            gbuf[source, j] = lax.dot_general(
                dy_ref[source, j], w_ref[j], (((1,), (1,)), ((), ())),
                preferred_element_type=jnp.float32,
            ).astype(gbuf.dtype)

    grads_of(lax.rem(col + 1, owners))
    barrier = pltpu.get_barrier_semaphore()
    for peer in range(owners - 1):
        other = lax.rem(col + 1 + peer, owners)
        pl.semaphore_signal(barrier, inc=1, device_id=(me, other), device_id_type=MESH)
    pl.semaphore_wait(barrier, owners - 1)

    def send(source, j):
        return pltpu.make_async_remote_copy(
            src_ref=gbuf.at[source, j],
            dst_ref=back_ref.at[col, j],
            send_sem=send_sem.at[source, j],
            recv_sem=recv_sem.at[col, j],
            device_id=(me, source),
            device_id_type=MESH,
        )

    def step(i, carry):
        grads_of(lax.rem(col + 1 + i, owners))
        previous = lax.rem(col + i, owners)
        for j in range(local_experts):
            send(previous, j).start()
        return carry

    lax.fori_loop(1, owners, step, 0)
    own = pltpu.make_async_copy(gbuf.at[col], back_ref.at[col], own_sem)
    own.start()

    def finish(peer, carry):
        other = lax.rem(col + 1 + peer, owners)
        for j in range(local_experts):
            send(other, j).wait_send()
        for j in range(local_experts):
            pltpu.make_async_remote_copy(
                src_ref=gbuf.at[other, j],
                dst_ref=back_ref.at[other, j],
                send_sem=send_sem.at[other, j],
                recv_sem=recv_sem.at[other, j],
                device_id=(me, other),
                device_id_type=MESH,
            ).wait_recv()
        return carry

    lax.fori_loop(0, owners - 1, finish, 0)
    own.wait()


def give_back(dy, full_down, owners):
    sources, local_experts, capacity, width = dy.shape
    hidden_units = full_down.shape[1]
    shape = (sources, local_experts, capacity, hidden_units)
    return pl.pallas_call(
        lambda *refs: return_kernel(owners, *refs),
        out_shape=jax.ShapeDtypeStruct(shape, dy.dtype),
        in_specs=[pl.BlockSpec(memory_space=pltpu.VMEM)] * 2,
        out_specs=pl.BlockSpec(memory_space=pl.ANY),
        scratch_shapes=[
            pltpu.VMEM(shape, dy.dtype),
            pltpu.SemaphoreType.DMA(()),
            pltpu.SemaphoreType.DMA((owners, local_experts)),
            pltpu.SemaphoreType.DMA((owners, local_experts)),
        ],
        compiler_params=pltpu.CompilerParams(
            collective_id=1, has_side_effects=True, vmem_limit_bytes=48 * 1024 * 1024
        ),
        cost_estimate=pl.CostEstimate(
            flops=2 * sources * local_experts * capacity * width * hidden_units,
            bytes_accessed=(dy.size + full_down.size + 2 * sources * local_experts * capacity * hidden_units) * 2,
            transcendentals=0,
        ),
    )(dy, full_down)


def slot_counts(ids, experts):
    routes = ids.shape[-1]
    onehot = (ids[..., None] == jnp.arange(experts, dtype=jnp.int32)).astype(jnp.bfloat16)
    lower = (jnp.arange(routes)[:, None] > jnp.arange(routes)[None, :]).astype(jnp.bfloat16)
    before = jnp.einsum("rq,...qe->...re", lower, onehot, preferred_element_type=jnp.float32)
    return jnp.sum(before * onehot.astype(jnp.float32), axis=-1).astype(jnp.int32)


def local(cotangent, saved_gate_up, route_ids, route_weights, w_down):
    tokens, top = route_ids.shape
    width = cotangent.shape[1]
    hidden_units = saved_gate_up.shape[2] // 2
    owners = lax.axis_size("expert")
    replicas = lax.axis_size("dp")
    me = lax.axis_index("expert")
    local_experts = w_down.shape[0]
    experts = local_experts * owners
    capacity = min(tokens, 2 * tokens * top // experts)
    routes = tokens * top

    cot_group = lax.all_gather(cotangent, "expert", axis=0, tiled=True)

    gate = saved_gate_up[:, :, :hidden_units].astype(jnp.float32)
    up = saved_gate_up[:, :, hidden_units:].astype(jnp.float32)
    sig = jax.nn.sigmoid(gate)
    act = gate * sig
    hidden = (act * up).astype(jnp.bfloat16)
    weights = route_weights[:, :, None]
    scaled = (weights * hidden.astype(jnp.float32)).astype(jnp.bfloat16)

    flat_ids = route_ids.reshape(routes)
    slot = slot_counts(flat_ids, experts)
    position = flat_ids * capacity + slot
    slot_ids = jnp.arange(experts * capacity, dtype=jnp.int32)
    match = position[None, :] == slot_ids[:, None]
    route_of_slot = jnp.sum(jnp.where(match, jnp.arange(routes, dtype=jnp.int32)[None, :], 0), axis=1)
    filled = jnp.any(match, axis=1)
    h_rows = jnp.dot(match.astype(jnp.bfloat16), scaled.reshape(routes, hidden_units),
                     preferred_element_type=jnp.bfloat16)
    h_send = h_rows.reshape(owners, local_experts, capacity, hidden_units)

    t_send = jnp.where(filled, route_of_slot // top, -1).reshape(owners, 1, local_experts * capacity)
    full_down, h_got, t_got = exchange(w_down, h_send, t_send, replicas, owners)
    h_got, t_got, cot_group = lax.optimization_barrier((h_got, t_got, cot_group))
    pick = (t_got.reshape(owners, local_experts * capacity, 1)
            == jnp.arange(tokens, dtype=jnp.int32)[None, None, :]).astype(jnp.bfloat16)
    dy = jnp.einsum(
        "sct,std->scd", pick, cot_group.reshape(owners, tokens, width),
        preferred_element_type=jnp.bfloat16,
    ).reshape(owners, local_experts, capacity, width)

    parts = []
    for j in range(local_experts):
        part = jnp.einsum(
            "scf,scd->fd", h_got[:, j], dy[:, j], preferred_element_type=jnp.float32
        ).astype(jnp.bfloat16)
        parts.append(part.reshape(replicas, hidden_units // replicas, width))
    stacked = jnp.stack(parts, axis=1)
    stacked, dy = lax.optimization_barrier((stacked, dy))
    summed = lax.psum_scatter(stacked, "dp", scatter_dimension=0, tiled=True)
    grad_down = summed[0].astype(jnp.float32)
    back = give_back(dy, full_down.reshape(local_experts, hidden_units, width), owners)
    take = (position.reshape(tokens, top, 1)
            == jnp.arange(experts * capacity, dtype=jnp.int32)[None, None, :]).astype(jnp.bfloat16)
    qf = jnp.einsum(
        "tkr,rf->tkf", take, back.reshape(experts * capacity, hidden_units),
        preferred_element_type=jnp.float32,
    )
    route_grad = jnp.sum(qf * hidden.astype(jnp.float32), -1)
    d_hidden = weights * qf
    d_gate = d_hidden * up * sig * (1.0 + gate * (1.0 - sig))
    d_up = d_hidden * act
    grad_gate_up = jnp.concatenate([d_gate, d_up], -1).astype(jnp.bfloat16)
    return (grad_gate_up, route_grad, grad_down)


def solution(mesh):
    return jax.shard_map(
        local,
        mesh=mesh,
        in_specs=(
            P(("dp", "expert"), None),
            P(("dp", "expert"), None, None),
            P(("dp", "expert"), None),
            P(("dp", "expert"), None),
            P("expert", "dp", None),
        ),
        out_specs=(
            P(("dp", "expert"), None, None),
            P(("dp", "expert"), None),
            P("expert", "dp", None),
        ),
        check_vma=False,
    )
```
